32 devices in a mesh: lm: 8 (over z, x), kf: 4 (over y, core).
Axes of the slice: x: 2, y: 2, z: 4, core: 2. Of those that a mesh axis runs over, the one named last changes fastest.
Arguments:
- residual_rows: bfloat16 [4096, 128], P(('lm', 'kf')), may hold values from -6 to 6
- jacobian: bfloat16 [4096, 15, 128], P(('lm', 'kf')), may hold values from -1.5 to 1.5
- nullspace: bfloat16 [4096, 128, 128], P(('lm', 'kf')), may hold values from -0.5 to 0.5
- frame_ids: int32 [4096, 64], P(('lm', 'kf')), may hold values from 0 to 16383, as said below
- obs_count: int32 [4096], P(('lm', 'kf')), may hold values from 4 to 64
- damping: float32 [15, 16384], P(None, 'kf'), may hold values from 1 to 10
- jacobi_scale: float32 [15, 16384], P(None, 'kf'), may hold values from 0.02 to 0.3
Outputs:
- solution: float32 [15, 16384], P(None, 'kf')
- residual: float32 [15, 16384], P(None, 'kf')
The draws below stay inside these ranges and needn't reach their ends.
Inputs may be any that keep to these rules, and one draw needn't show every extreme that they name: `frame_ids`: within a block the keyframe ids rise strictly from slot to slot by 1 to 8. A block stored on the device with kf index w names only keyframes from 4096 * w up to but not including 4096 * (w + 2), and never one of 16384 or more.
All inputs are finite; a program needn't handle non-finite values.
Results may differ from the reference program's by a relative error of at most 0.005.
Values sent between devices are 32-bit elements; how exact they have to be, the bound alone decides.
A program may use at most 64 MiB of HBM per device.

```python
import math
import jax
import jax.numpy as jnp
from jax import lax

STATE = 15
OBS = 64
ROWS = 128
STEP_MAX = 8
KF_DEV = 4096
BLK_DEV = 128
ITERS = 2
NK = 16384
NB = 4096
N_KF = 4


def draw_frame_ids(key, part):
    key_base = jax.random.fold_in(key, 11)
    key_gaps = jax.random.fold_in(key, 12)
    blocks = jnp.arange(NB, dtype=jnp.int32)
    window = blocks // BLK_DEV % N_KF
    limit = jnp.where(window == N_KF - 1, KF_DEV - STEP_MAX * OBS, KF_DEV)
    base = jax.random.randint(key_base, (NB,), 0, limit)
    gaps = jax.random.randint(key_gaps, (NB, OBS), 1, STEP_MAX + 1)
    offsets = jnp.cumsum(gaps, axis=1) - gaps[:, :1]
    last_base = KF_DEV - 1 - offsets[:, -1]
    base = jnp.where(blocks == 0, 0, base)
    base = jnp.where(blocks == NB - 1, last_base, base)
    return (window * KF_DEV + base)[:, None] + offsets


def touch_ends(result, stream_key, least, high):
    longest = result.shape.index(max(result.shape))
    spots = []
    for shift in (0, 1):
        where = [jax.random.randint(jax.random.fold_in(stream_key, axis), (), 0, length) for axis, length in enumerate(result.shape)]
        where[longest] = (where[longest] + shift) % result.shape[longest]
        spots.append(tuple(where))
    return result.at[spots[0]].set(least).at[spots[1]].set(high)


def block_scale(key, dims, cuts, smallest, top_value):
    level = 1.0
    for axis_at, blocks in cuts:
        draws = jax.random.uniform(jax.random.fold_in(jax.random.fold_in(key, 6), axis_at), (blocks,), jnp.float32, smallest / len(cuts), top_value / len(cuts))
        level = level * jnp.repeat(jnp.exp(draws), dims[axis_at] // blocks).reshape((-1,) + (1,) * (len(dims) - 1 - axis_at))
    return level


def gaussian(own_key, extent, scale, most, cuts=(), kind=jnp.bfloat16):
    result = jax.random.normal(own_key, extent, jnp.float32) * scale
    if len(cuts) > 0:
        result = block_scale(own_key, extent, cuts, -0.22, 0.18) * result
    return jnp.clip(result, min=-most, max=most).astype(kind)


def setup_inputs(seed: int = 0) -> dict:
    splits = jax.random.split(jax.random.key(seed), 8)
    residual_rows = gaussian(splits[0], (NB, ROWS), 1.0, 6.0, ((0, 32),))
    jacobian = gaussian(splits[1], (NB, STATE, ROWS), STATE ** -0.5, 1.5, ((0, 32),))
    nullspace = gaussian(splits[2], (NB, ROWS, ROWS), ROWS ** -0.5, 0.5, ((0, 32),))
    frame_ids = draw_frame_ids(jax.random.fold_in(splits[7], 71), 0)
    obs_count = touch_ends(jax.random.randint(splits[4], (NB,), 4, OBS + 1), jax.random.fold_in(splits[4], 1), 4, OBS).astype(jnp.int32)
    damping = jnp.clip(jnp.exp(math.log(10.0) - 2.3025851 * jax.random.uniform(splits[5], (STATE, NK), jnp.float32) ** block_scale(splits[5], (STATE, NK), ((1, 4),), -0.2, 0.2)), 1.0, 10.0)
    jacobi_scale = jnp.clip(jnp.exp(math.log(0.3) - 2.7080503 * jax.random.uniform(splits[6], (STATE, NK), jnp.float32) ** block_scale(splits[6], (STATE, NK), ((1, 4),), -0.2, 0.2)), 0.02, 0.3)
    return {"residual_rows": residual_rows, "jacobian": jacobian, "nullspace": nullspace, "frame_ids": frame_ids, "obs_count": obs_count, "damping": damping, "jacobi_scale": jacobi_scale}


def row_layout(frame_ids, obs_count):
    slots = lax.broadcasted_iota(jnp.int32, frame_ids.shape, 1)
    live = (slots < obs_count[:, None]).astype(jnp.float32)
    return jnp.repeat(frame_ids, 2, axis=1), jnp.repeat(live, 2, axis=1)


def project(lifted, nullspace, live):
    lifted_half = (lifted * live).astype(jnp.bfloat16).astype(jnp.float32)
    factor = nullspace.astype(jnp.float32)
    inner = jnp.einsum('brk,br->bk', factor, lifted_half).astype(jnp.bfloat16).astype(jnp.float32)
    spread = jnp.einsum('brk,bk->br', factor, inner)
    return spread * live


def accumulate(field, use_field, residual_rows, jacobian, nullspace, frame_ids, obs_count):
    groups = NB // BLK_DEV

    def split(arr):
        return arr.reshape((groups, BLK_DEV) + arr.shape[1:])

    def one_group(total, pieces):
        rows_res, jac_part, null_part, ids_part, count_part = pieces
        row_ids, live = row_layout(ids_part, count_part)
        if use_field:
            gathered = jnp.take(field, row_ids, axis=1)
            lifted = jnp.sum(jac_part.astype(jnp.float32) * jnp.moveaxis(gathered, 0, 1), axis=1)
        else:
            lifted = rows_res.astype(jnp.float32)
        spread = project(lifted, null_part, live)
        terms = jac_part.astype(jnp.float32) * spread[:, None, :]
        terms = jnp.moveaxis(terms, 1, 0).reshape(STATE, -1)
        return total.at[:, row_ids.reshape(-1)].add(terms), None

    start = jnp.zeros((STATE, NK), jnp.float32)
    pieces = (split(residual_rows), split(jacobian), split(nullspace), split(frame_ids), split(obs_count))
    total, unused = lax.scan(one_group, start, pieces)
    return total


def reference(residual_rows, jacobian, nullspace, frame_ids, obs_count, damping, jacobi_scale):
    gradient = -accumulate(None, False, residual_rows, jacobian, nullspace, frame_ids, obs_count)
    residual = gradient
    solution = jnp.zeros_like(gradient)
    scaled = jacobi_scale * residual
    direction = scaled
    energy = jnp.sum(residual * scaled)
    for step_index in range(ITERS):
        applied = accumulate(direction, True, residual_rows, jacobian, nullspace, frame_ids, obs_count) + damping * direction
        step_size = energy / jnp.sum(direction * applied)
        solution = solution + step_size * direction
        residual = residual - step_size * applied
        if step_index + 1 < ITERS:
            scaled = jacobi_scale * residual
            fresh = jnp.sum(residual * scaled)
            direction = scaled + (fresh / energy) * direction
            energy = fresh
    return solution, residual
```

```python
import functools

import jax
import jax.numpy as jnp
from jax import lax
from jax.experimental import pallas as pl
from jax.experimental.pallas import tpu as pltpu
from jax.sharding import PartitionSpec as P

ITERS = 2
LANES = 128
PAD = 16
SPAN = 5
CHUNK = 32
PICK = 8
DEAD = 1 << 20
LIMIT = 16 << 20


def spread_over(lifted, factors, first):
    picks = lax.broadcasted_iota(jnp.int32, lifted.shape, 0)
    half = lifted.astype(jnp.bfloat16)
    inner = jnp.zeros(lifted.shape, jnp.float32)
    for i in range(PICK):
        inner = jnp.where(picks == i, jnp.dot(half, factors[first + i], preferred_element_type=jnp.float32), inner)
    half = inner.astype(jnp.bfloat16)
    spread = jnp.zeros(lifted.shape, jnp.float32)
    for i in range(PICK):
        spread = jnp.where(
            picks == i,
            lax.dot_general(
                half, factors[first + i], (((1,), (1,)), ((), ())), preferred_element_type=jnp.float32
            ),
            spread,
        )
    return spread


def sums_of_eight(tiles):
    rows = lax.broadcasted_iota(jnp.int32, tiles[0].shape, 0)
    width = 1
    while width < PICK:
        low = (rows & width) == 0
        tiles = [
            jnp.where(low, left, right) + pltpu.roll(jnp.where(low, right, left), width, axis=0)
            for left, right in zip(tiles[::2], tiles[1::2])
        ]
        width *= 2
    return tiles[0]


def along_lanes(tile, lanes):
    return jnp.take_along_axis(tile, lanes, axis=1, mode="promise_in_bounds")


def scatter_terms(starts, block, i, jac, row_ref, inv_ref, out_ref, even):
    terms = jac * row_ref[pl.ds(i, 1), :]
    terms = jnp.where(even, terms + pltpu.roll(terms, LANES - 1, axis=1), 0.0)
    begin = starts[block]
    for q in range(SPAN):
        lanes = jnp.broadcast_to(inv_ref[i, pl.ds(q, 1), :], terms.shape)
        out_ref[begin + q] += along_lanes(terms, lanes)


def even_lanes():
    return (lax.broadcasted_iota(jnp.int32, (PAD, LANES), 1) & 1) == 0


def product_kernel(starts, field_ref, code_ref, inv_ref, jac_ref, null_ref, out_ref, row_ref):
    out_ref[...] = jnp.zeros_like(out_ref)
    even = even_lanes()

    @pl.loop(0, null_ref.shape[0] // CHUNK)
    def _(step):
        base = pl.multiple_of(step * CHUNK, CHUNK)
        mine = pl.ds(base, CHUNK)
        codes, invs, jacs, factors = code_ref.at[mine], inv_ref.at[mine], jac_ref.at[mine], null_ref.at[mine]
        for first in range(0, CHUNK, PICK):
            tiles = []
            for i in range(first, first + PICK):
                begin = starts[base + i]
                code = jnp.broadcast_to(codes[pl.ds(i, 1), :], (PAD, LANES))
                lanes, part = code & (LANES - 1), code >> 7
                gathered = jnp.zeros((PAD, LANES), jnp.float32)
                for q in range(SPAN):
                    gathered = jnp.where(part == q, along_lanes(field_ref[begin + q], lanes), gathered)
                gathered = gathered * jacs[i]
                tiles.append(gathered[:PICK] + gathered[PICK:])
            row_ref[pl.ds(first, PICK), :] = spread_over(sums_of_eight(tiles), factors, first)
        for i in range(CHUNK):
            scatter_terms(starts, base + i, i, jacs[i], row_ref, invs, out_ref, even)


def gradient_kernel(
    starts, ids_ref, count_ref, rows_ref, jac_in, null_in,
    out_ref, code_ref, inv_ref, jac_ref, null_ref, row_ref, slot_ref, sems,
):
    blocks = null_ref.shape[0]
    chunks = blocks // CHUNK
    copies = []
    for c in range(chunks):
        mine = pl.ds(c * CHUNK, CHUNK)
        copies.append(pltpu.make_async_copy(null_in.at[mine], null_ref.at[mine], sems.at[c]))
        copies[c].start()
    out_ref[...] = jnp.zeros_like(out_ref)
    frames = out_ref.shape[0] // 2 * LANES
    ids = ids_ref[...] - lax.axis_index("kf") * frames
    begin = jnp.minimum(ids[:1] >> 7, out_ref.shape[0] - SPAN)
    slots = lax.broadcasted_iota(jnp.int32, ids.shape, 0)
    ids = jnp.where(slots < count_ref[...], ids - begin * LANES, DEAD)
    offs = jnp.transpose(jnp.concatenate([ids] * (LANES // ids.shape[0]), axis=0))
    slot_ref[...] = offs
    lanes = lax.broadcasted_iota(jnp.int32, offs.shape, 1)
    code_ref[...] = along_lanes(offs, lanes >> 1)
    state = jac_in.shape[0]
    for c in range(PAD):
        for g in range(blocks // PICK):
            spot = pl.ds(g * PICK * PAD + c, PICK, stride=PAD)
            if c < state:
                jac_ref[spot, :] = jac_in[c, pl.ds(g * PICK, PICK), :].astype(jnp.float32)
            else:
                jac_ref[spot, :] = jnp.zeros((PICK, LANES), jnp.float32)
    even = even_lanes()
    tile = (PICK, LANES)
    target = lax.broadcasted_iota(jnp.int32, tile, 0) * LANES + lax.broadcasted_iota(jnp.int32, tile, 1)
    for c in range(chunks):
        copies[c].wait()

    @pl.loop(0, chunks)
    def _(step):
        base = pl.multiple_of(step * CHUNK, CHUNK)
        mine = pl.ds(base, CHUNK)
        codes, invs, factors = code_ref.at[mine], inv_ref.at[mine], null_ref.at[mine]
        offsets = slot_ref.at[mine]
        jacs = jac_ref.at[pl.ds(pl.multiple_of(step * CHUNK * PAD, CHUNK * PAD), CHUNK * PAD)]
        residuals = rows_ref[mine, :].astype(jnp.float32)
        lifted = jnp.where(codes[...] < DEAD, residuals, 0.0)
        for first in range(0, CHUNK, PICK):
            row_ref[pl.ds(first, PICK), :] = spread_over(lifted[first:first + PICK], factors, first)
        for i in range(CHUNK):
            offset = jnp.broadcast_to(offsets[pl.ds(i, 1), :], tile)
            at = jnp.zeros(tile, jnp.int32)
            width = ids_ref.shape[0] // 2
            while width > 0:
                at = jnp.where(along_lanes(offset, at + width) <= target, at + width, at)
                width //= 2
            invs[i] = jnp.where(along_lanes(offset, at) == target, 2 * at, LANES - 1)
        for i in range(CHUNK):
            scatter_terms(starts, base + i, i, jacs[pl.ds(i * PAD, PAD), :], row_ref, invs, out_ref, even)


def local_call(kernel, name, outs, extra, in_specs, *operands):
    vmem = pl.BlockSpec(memory_space=pltpu.VMEM)
    return pl.pallas_call(
        kernel,
        in_specs=[pl.BlockSpec(memory_space=pltpu.SMEM)] + in_specs,
        out_specs=[vmem] * len(outs),
        out_shape=outs,
        scratch_shapes=[pltpu.VMEM((CHUNK, LANES), jnp.float32)] + extra,
        compiler_params=pltpu.CompilerParams(vmem_limit_bytes=LIMIT),
        name=name,
    )(*operands)


def remote(src, dst, send, recv, axis, index):
    return pltpu.make_async_remote_copy(
        src_ref=src, dst_ref=dst, send_sem=send, recv_sem=recv,
        device_id={axis: index}, device_id_type=pl.DeviceIdType.MESH,
    )


def greet(n, m):
    i, w = lax.axis_index("lm"), lax.axis_index("kf")
    barrier = pltpu.get_barrier_semaphore()
    for k in range(1, n):
        pl.semaphore_signal(
            barrier, inc=1, device_id={"lm": lax.rem(i + k, n)}, device_id_type=pl.DeviceIdType.MESH
        )
    for k in range(1, m):
        pl.semaphore_signal(
            barrier, inc=1, device_id={"kf": lax.rem(w + k, m)}, device_id_type=pl.DeviceIdType.MESH
        )
    pl.semaphore_wait(barrier, n - 1 + m - 1)


def reduce_spread(n, m, pair, h, full, bufs, sems):
    fold, acc, rs = bufs
    fold_s, fold_r, rs_s, rs_r, ag_s, ag_r, fw_s, fw_r = sems
    own = acc.shape[0]
    sh = own // n
    i, w = lax.axis_index("lm"), lax.axis_index("kf")
    later, former = lax.rem(w + 1, m), lax.rem(w + m - 1, m)

    def at(ref, j, base=0):
        return ref.at[pl.ds(base + j * sh, sh)]

    order = [lax.rem(i + k, n) for k in range(1, n)] + [i]
    others = order[:-1]
    folds = [remote(at(h, j, own), at(fold, j), fold_s.at[k], fold_r.at[k], "kf", later) for k, j in enumerate(order)]

    @pl.when(w < m - 1)
    def _():
        for copy in folds:
            copy.start()

    scatters = [remote(at(acc, j), rs.at[i], rs_s.at[k], rs_r.at[i], "lm", j) for k, j in enumerate(others)]
    for k, j in enumerate(order):
        spot = pl.ds(j * sh, sh)

        @pl.when(w > 0)
        def _():
            folds[k].wait_recv()
            acc[spot] = h[spot] + fold[spot]

        @pl.when(w == 0)
        def _():
            acc[spot] = h[spot]

        if k < n - 1:
            scatters[k].start()
    total = acc[pl.ds(i * sh, sh)]
    arrive = [lax.rem(i + n - k, n) for k in range(1, n)]
    for j in arrive:
        remote(at(acc, j), rs.at[j], rs_s.at[0], rs_r.at[j], "lm", j).wait_recv()
        total = total + rs[j]
    full[pl.ds(i * sh, sh)] = total
    gathers = [remote(at(full, i), at(full, i), ag_s.at[k], ag_r.at[i], "lm", j) for k, j in enumerate(others)]
    for copy in gathers:
        copy.start()
    forwards = []
    for k, j in enumerate([i] + arrive):
        if k > 0:
            remote(at(full, j), at(full, j), ag_s.at[0], ag_r.at[j], "lm", j).wait_recv()
        if pair:
            copy = remote(at(full, j), at(full, j, own), fw_s.at[k], fw_r.at[k], "kf", former)
            forwards.append(copy)

            @pl.when(w > 0)
            def _():
                copy.start()

    def finish_pair():
        @pl.when(w < m - 1)
        def _():
            for copy in forwards:
                copy.wait_recv()

        @pl.when(w == m - 1)
        def _():
            full[pl.ds(own, own)] = jnp.zeros((own,) + full.shape[1:], jnp.float32)

    def finish_sends():
        @pl.when(w < m - 1)
        def _():
            for copy in folds:
                copy.wait_send()

        for copy in scatters + gathers:
            copy.wait_send()
        if pair:

            @pl.when(w > 0)
            def _():
                for copy in forwards:
                    copy.wait_send()

    return finish_pair, finish_sends


def over_windows(m, value, slots, send, recv):
    w = lax.axis_index("kf")
    slots[w] = jnp.sum(value, axis=0)
    copies = []
    for k in range(1, m):
        copy = remote(slots.at[w], slots.at[w], send.at[k], recv.at[w], "kf", lax.rem(w + k, m))
        copy.start()
        copies.append(copy)
    for k in range(1, m):
        j = lax.rem(w + k, m)
        remote(slots.at[j], slots.at[j], send.at[0], recv.at[j], "kf", j).wait_recv()
    total = slots[0]
    for j in range(1, m):
        total = total + slots[j]

    def finish():
        for copy in copies:
            copy.wait_send()

    return jnp.sum(jnp.sum(total, axis=0, keepdims=True), axis=1, keepdims=True), finish


def columns(g):
    return pl.ds(g * LANES, LANES)


def first_phase(n, m, h, damping, jacobi_scale, res_out, dir_out, energy_out, diag_out, full, fold, acc, rs, slots, diag, *sems):
    own = acc.shape[0]
    state = damping.shape[0]
    w = lax.axis_index("kf")
    diag[...] = jnp.zeros_like(diag)
    for g in range(own):
        diag[g, pl.ds(0, state), :] = damping[:, columns(g)]
        diag[g, pl.ds(PAD, state), :] = jacobi_scale[:, columns(g)]
    greet(n, m)
    diag_copy = remote(
        diag.at[pl.ds(0, own)], diag.at[pl.ds(own, own)], sems[10].at[0], sems[10].at[1], "kf", lax.rem(w + m - 1, m)
    )

    @pl.when(w > 0)
    def _():
        diag_copy.start()

    finish_pair, finish_sends = reduce_spread(n, m, True, h, full, (fold, acc, rs), sems[:8])
    grad = full[pl.ds(0, own)]
    scale = diag[pl.ds(0, own), pl.ds(PAD, PAD), :]
    energy, finish = over_windows(m, grad * grad * scale, slots.at[0], sems[8].at[0], sems[9].at[0])
    energy_out[...] = jnp.broadcast_to(energy, energy_out.shape)
    finish_pair()

    @pl.when(w < m - 1)
    def _():
        diag_copy.wait_recv()

    @pl.when(w > 0)
    def _():
        diag_copy.wait_send()

    res_out[...] = -full[...]
    dir_out[...] = -full[...] * diag[:, pl.ds(PAD, PAD), :]
    diag_out[...] = diag[...]
    finish()
    finish_sends()


def middle_phase(begun, n, m, h, res, direction, diag, energy_in, *rest):
    if begun:
        answer_in, *rest = rest
    res_out, dir_out, energy_out, answer_out, full, fold, acc, rs, slots, *sems = rest
    own = acc.shape[0]
    here, damp, scale = pl.ds(0, own), pl.ds(0, PAD), pl.ds(PAD, PAD)
    greet(n, m)
    finish_pair, finish_sends = reduce_spread(n, m, True, h, full, (fold, acc, rs), sems[:8])
    energy = energy_in[pl.ds(0, 1), pl.ds(0, 1)]
    applied = full[here] + diag[here, damp, :] * direction[here]
    curve, finish_a = over_windows(m, direction[here] * applied, slots.at[0], sems[8].at[0], sems[9].at[0])
    step = energy / curve
    after = res[here] - step * applied
    fresh, finish_b = over_windows(m, after * after * diag[here, scale, :], slots.at[1], sems[8].at[1], sems[9].at[1])
    gained = step * direction[here]
    answer_out[...] = answer_in[...] + gained if begun else gained
    energy_out[...] = jnp.broadcast_to(fresh, energy_out.shape)
    finish_pair()
    after = res[...] - step * (full[...] + diag[:, damp, :] * direction[...])
    res_out[...] = after
    dir_out[...] = diag[:, scale, :] * after + fresh / energy * direction[...]
    finish_a()
    finish_b()
    finish_sends()


def last_phase(n, m, h, direction, diag, energy_in, applied_out, step_out, full, fold, acc, rs, slots, *sems):
    own = acc.shape[0]
    here = pl.ds(0, own)
    greet(n, m)
    _, finish_sends = reduce_spread(n, m, False, h, full, (fold, acc, rs), sems[:8])
    applied = full[here] + diag[here, pl.ds(0, PAD), :] * direction[here]
    applied_out[...] = applied
    curve, finish = over_windows(m, direction[here] * applied, slots.at[0], sems[8].at[0], sems[9].at[0])
    step = energy_in[pl.ds(0, 1), pl.ds(0, 1)] / curve
    step_out[...] = jnp.broadcast_to(step, step_out.shape)
    finish()
    finish_sends()


def update_kernel(res, direction, applied, answer_in, step_in, answer_out, res_out):
    own = applied.shape[0]
    state = res_out.shape[0]
    step = step_in[pl.ds(0, 1), pl.ds(0, 1)]
    for g in range(own):
        answer_out[:, columns(g)] = (answer_in[g] + step * direction[g])[:state]
        res_out[:, columns(g)] = (res[g] - step * applied[g])[:state]


def last_update(shape, res, direction, applied, answer, step):
    half = pl.BlockSpec(applied.shape, lambda i: (0, 0, 0))
    whole = pl.BlockSpec(shape, lambda i: (0, 0))
    return pl.pallas_call(
        update_kernel,
        grid=(1,),
        in_specs=[half] * 4 + [pl.BlockSpec(step.shape, lambda i: (0, 0))],
        out_specs=[whole] * 2,
        out_shape=[jax.ShapeDtypeStruct(shape, jnp.float32)] * 2,
        compiler_params=pltpu.CompilerParams(vmem_limit_bytes=LIMIT),
        name="last_update",
    )(res, direction, applied, answer, step)


def phase(kernel, name, number, n, m, outs, extra, *operands):
    pair = operands[0].shape
    own = pair[0] // 2
    tile = pair[1:]
    vmem = pl.BlockSpec(memory_space=pltpu.VMEM)
    dma = pltpu.SemaphoreType.DMA
    return pl.pallas_call(
        functools.partial(kernel, n, m),
        in_specs=[vmem] * len(operands),
        out_specs=[vmem] * len(outs),
        out_shape=[jax.ShapeDtypeStruct(shape, jnp.float32) for shape in outs],
        scratch_shapes=[
            pltpu.VMEM(pair, jnp.float32),
            pltpu.VMEM((own,) + tile, jnp.float32),
            pltpu.VMEM((own,) + tile, jnp.float32),
            pltpu.VMEM((n, own // n) + tile, jnp.float32),
            pltpu.VMEM((2, m) + tile, jnp.float32),
        ]
        + [pltpu.VMEM(shape, jnp.float32) for shape in extra]
        + [dma((n,))] * 8
        + [dma((2, m))] * 2
        + [dma((2,))],
        compiler_params=pltpu.CompilerParams(collective_id=number, has_side_effects=True, vmem_limit_bytes=LIMIT),
        name=name,
    )(*operands)


def shards(residual_rows, jacobian, nullspace, frame_ids, obs_count, damping, jacobi_scale):
    state, frames = damping.shape
    own = frames // LANES
    blocks = nullspace.shape[0]
    starts = jnp.minimum((frame_ids[:, 0] - lax.axis_index("kf") * frames) >> 7, 2 * own - SPAN)
    n, m = lax.axis_size("lm"), lax.axis_size("kf")
    pair, one, tile = (2 * own, PAD, LANES), (own, PAD, LANES), (8, LANES)
    both = (2 * own, 2 * PAD, LANES)
    vmem = pl.BlockSpec(memory_space=pltpu.VMEM)
    gradient, code, inverse, jac, null = local_call(
        gradient_kernel, "local_gradient",
        [
            jax.ShapeDtypeStruct(pair, jnp.float32),
            jax.ShapeDtypeStruct((blocks, LANES), jnp.int32),
            jax.ShapeDtypeStruct((blocks, PICK, LANES), jnp.int32),
            jax.ShapeDtypeStruct((blocks * PAD, LANES), jnp.float32),
            jax.ShapeDtypeStruct(nullspace.shape, nullspace.dtype),
        ],
        [pltpu.VMEM((blocks, LANES), jnp.int32), pltpu.SemaphoreType.DMA((blocks // CHUNK,))],
        [vmem] * 4 + [pl.BlockSpec(memory_space=pltpu.HBM)],
        starts, jnp.transpose(frame_ids), obs_count[None, :], residual_rows,
        jnp.transpose(jacobian, (1, 0, 2)), nullspace,
    )
    jac = jac.reshape(blocks, PAD, LANES)

    def product(field):
        return local_call(
            product_kernel, "local_field", [jax.ShapeDtypeStruct(pair, jnp.float32)], [], [vmem] * 5,
            starts, field, code, inverse, jac, null,
        )[0]

    residual, direction, energy, diag = phase(
        first_phase, "first_phase", 0, n, m, (pair, pair, tile, both), (both,), gradient, damping, jacobi_scale
    )
    answer = ()
    for number in range(1, ITERS):
        residual, direction, energy, *answer = phase(
            functools.partial(middle_phase, number > 1), "middle_phase", number, n, m, (pair, pair, tile, one), (),
            product(direction), residual, direction, diag, energy, *answer,
        )
    applied, step = phase(
        last_phase, "last_phase", ITERS, n, m, (one, tile), (), product(direction), direction, diag, energy
    )
    return tuple(last_update(damping.shape, residual, direction, applied, *answer, step))


def solution(mesh):
    placed = (
        P(("lm", "kf"), None),
        P(("lm", "kf"), None, None),
        P(("lm", "kf"), None, None),
        P(("lm", "kf"), None),
        P(("lm", "kf")),
        P(None, "kf"),
        P(None, "kf"),
    )
    return jax.shard_map(
        shards,
        mesh=mesh,
        in_specs=placed,
        out_specs=(P(None, "kf"), P(None, "kf")),
        check_vma=False,
    )
```

```python
import functools

import jax
import jax.numpy as jnp
from jax import lax
from jax.experimental import pallas as pl
from jax.experimental.pallas import tpu as pltpu
from jax.sharding import PartitionSpec as P

ITERS = 2
LANES = 128
PAD = 16
SPAN = 5
CHUNK = 32
PICK = 8
DEAD = 1 << 20
LIMIT = 16 << 20


def spread_over(lifted, factors, first):
    picks = lax.broadcasted_iota(jnp.int32, lifted.shape, 0)
    half = lifted.astype(jnp.bfloat16)
    inner = jnp.zeros(lifted.shape, jnp.float32)
    for i in range(PICK):
        inner = jnp.where(picks == i, jnp.dot(half, factors[first + i], preferred_element_type=jnp.float32), inner)
    half = inner.astype(jnp.bfloat16)
    spread = jnp.zeros(lifted.shape, jnp.float32)
    for i in range(PICK):
        spread = jnp.where(
            picks == i,
            lax.dot_general(
                half, factors[first + i], (((1,), (1,)), ((), ())), preferred_element_type=jnp.float32
            ),
            spread,
        )
    return spread


def sums_of_eight(tiles):
    rows = lax.broadcasted_iota(jnp.int32, tiles[0].shape, 0)
    width = 1
    while width < PICK:
        low = (rows & width) == 0
        tiles = [
            jnp.where(low, left, right) + pltpu.roll(jnp.where(low, right, left), width, axis=0)
            for left, right in zip(tiles[::2], tiles[1::2])
        ]
        width *= 2
    return tiles[0]


def along_lanes(tile, lanes):
    return jnp.take_along_axis(tile, lanes, axis=1, mode="promise_in_bounds")


def scatter_terms(starts, block, i, jac, row_ref, inv_ref, out_ref, even):
    terms = jac * row_ref[pl.ds(i, 1), :]
    terms = jnp.where(even, terms + pltpu.roll(terms, LANES - 1, axis=1), 0.0)
    begin = starts[block]
    for q in range(SPAN):
        lanes = jnp.broadcast_to(inv_ref[i, pl.ds(q, 1), :], terms.shape)
        out_ref[begin + q] += along_lanes(terms, lanes)


def even_lanes():
    return (lax.broadcasted_iota(jnp.int32, (PAD, LANES), 1) & 1) == 0


def product_kernel(starts, field_ref, code_ref, inv_ref, jac_ref, null_ref, out_ref, row_ref):
    out_ref[...] = jnp.zeros_like(out_ref)
    even = even_lanes()

    @pl.loop(0, null_ref.shape[0] // CHUNK)
    def _(step):
        base = pl.multiple_of(step * CHUNK, CHUNK)
        mine = pl.ds(base, CHUNK)
        codes, invs, jacs, factors = code_ref.at[mine], inv_ref.at[mine], jac_ref.at[mine], null_ref.at[mine]
        for first in range(0, CHUNK, PICK):
            tiles = []
            for i in range(first, first + PICK):
                begin = starts[base + i]
                code = jnp.broadcast_to(codes[pl.ds(i, 1), :], (PAD, LANES))
                lanes, part = code & (LANES - 1), code >> 7
                gathered = jnp.zeros((PAD, LANES), jnp.float32)
                for q in range(SPAN):
                    gathered = jnp.where(part == q, along_lanes(field_ref[begin + q], lanes), gathered)
                gathered = gathered * jacs[i]
                tiles.append(gathered[:PICK] + gathered[PICK:])
            row_ref[pl.ds(first, PICK), :] = spread_over(sums_of_eight(tiles), factors, first)
        for i in range(CHUNK):
            scatter_terms(starts, base + i, i, jacs[i], row_ref, invs, out_ref, even)


def gradient_kernel(
    starts, ids_ref, count_ref, rows_ref, jac_in, null_in,
    out_ref, code_ref, inv_ref, jac_ref, null_ref, row_ref, slot_ref, sems,
):
    blocks = null_ref.shape[0]
    chunks = blocks // CHUNK
    copies = []
    for c in range(chunks):
        mine = pl.ds(c * CHUNK, CHUNK)
        copies.append(pltpu.make_async_copy(null_in.at[mine], null_ref.at[mine], sems.at[c]))
        copies[c].start()
    out_ref[...] = jnp.zeros_like(out_ref)
    frames = out_ref.shape[0] // 2 * LANES
    ids = ids_ref[...] - lax.axis_index("kf") * frames
    begin = jnp.minimum(ids[:1] >> 7, out_ref.shape[0] - SPAN)
    slots = lax.broadcasted_iota(jnp.int32, ids.shape, 0)
    ids = jnp.where(slots < count_ref[...], ids - begin * LANES, DEAD)
    offs = jnp.transpose(jnp.concatenate([ids] * (LANES // ids.shape[0]), axis=0))
    slot_ref[...] = offs
    lanes = lax.broadcasted_iota(jnp.int32, offs.shape, 1)
    code_ref[...] = along_lanes(offs, lanes >> 1)
    state = jac_in.shape[0]
    for c in range(PAD):
        for g in range(blocks // PICK):
            spot = pl.ds(g * PICK * PAD + c, PICK, stride=PAD)
            if c < state:
                jac_ref[spot, :] = jac_in[c, pl.ds(g * PICK, PICK), :].astype(jnp.float32)
            else:
                jac_ref[spot, :] = jnp.zeros((PICK, LANES), jnp.float32)
    even = even_lanes()
    tile = (PICK, LANES)
    target = lax.broadcasted_iota(jnp.int32, tile, 0) * LANES + lax.broadcasted_iota(jnp.int32, tile, 1)
    for c in range(chunks):
        copies[c].wait()

    @pl.loop(0, chunks)
    def _(step):
        base = pl.multiple_of(step * CHUNK, CHUNK)
        mine = pl.ds(base, CHUNK)
        codes, invs, factors = code_ref.at[mine], inv_ref.at[mine], null_ref.at[mine]
        offsets = slot_ref.at[mine]
        jacs = jac_ref.at[pl.ds(pl.multiple_of(step * CHUNK * PAD, CHUNK * PAD), CHUNK * PAD)]
        residuals = rows_ref[mine, :].astype(jnp.float32)
        lifted = jnp.where(codes[...] < DEAD, residuals, 0.0)
        for first in range(0, CHUNK, PICK):
            row_ref[pl.ds(first, PICK), :] = spread_over(lifted[first:first + PICK], factors, first)
        for i in range(CHUNK):
            offset = jnp.broadcast_to(offsets[pl.ds(i, 1), :], tile)
            at = jnp.zeros(tile, jnp.int32)
            width = ids_ref.shape[0] // 2
            while width > 0:
                at = jnp.where(along_lanes(offset, at + width) <= target, at + width, at)
                width //= 2
            invs[i] = jnp.where(along_lanes(offset, at) == target, 2 * at, LANES - 1)
        for i in range(CHUNK):
            scatter_terms(starts, base + i, i, jacs[pl.ds(i * PAD, PAD), :], row_ref, invs, out_ref, even)


def local_call(kernel, name, outs, extra, in_specs, *operands):
    vmem = pl.BlockSpec(memory_space=pltpu.VMEM)
    return pl.pallas_call(
        kernel,
        in_specs=[pl.BlockSpec(memory_space=pltpu.SMEM)] + in_specs,
        out_specs=[vmem] * len(outs),
        out_shape=outs,
        scratch_shapes=[pltpu.VMEM((CHUNK, LANES), jnp.float32)] + extra,
        compiler_params=pltpu.CompilerParams(vmem_limit_bytes=LIMIT),
        name=name,
    )(*operands)


def remote(src, dst, send, recv, axis, index):
    return pltpu.make_async_remote_copy(
        src_ref=src, dst_ref=dst, send_sem=send, recv_sem=recv,
        device_id={axis: index}, device_id_type=pl.DeviceIdType.MESH,
    )


def partner(i, k):
    bit, flipped = 1, i * 0
    while bit <= k or bit == 1:
        digit = lax.rem(i // bit, 2)
        flipped = flipped + bit * ((1 - 2 * digit) if k & bit else 0)
        bit *= 2
    return i + flipped


def greet(n, m):
    i, w = lax.axis_index("lm"), lax.axis_index("kf")
    barrier = pltpu.get_barrier_semaphore()
    for k in range(n - 1, 0, -1):
        pl.semaphore_signal(
            barrier, inc=1, device_id={"lm": partner(i, k)}, device_id_type=pl.DeviceIdType.MESH
        )
    for k in range(1, m):
        pl.semaphore_signal(
            barrier, inc=1, device_id={"kf": lax.rem(w + k, m)}, device_id_type=pl.DeviceIdType.MESH
        )
    return lambda: pl.semaphore_wait(barrier, n - 1 + m - 1)


def all_reduce(n, m, pair, h, full, bufs, sems, on_shard):
    fold, acc, rs, near, far = bufs
    fold_s, fold_r, rs_s, rs_r, ag_s, ag_r, fw_s, fw_r, near_s, near_r, far_s, far_r = sems
    own = acc.shape[0]
    sh = own // n
    i, w = lax.axis_index("lm"), lax.axis_index("kf")
    later, former = lax.rem(w + 1, m), lax.rem(w + m - 1, m)

    def at(ref, j, base=0):
        return ref.at[pl.ds(base + j * sh, sh)]

    peers = [partner(i, k) for k in range(n)]
    outward = range(n - 1, 0, -1)
    folds = {
        k: remote(at(h, peers[k], own), at(fold, peers[k]), fold_s.at[k], fold_r.at[k], "kf", later) for k in range(n)
    }

    @pl.when(w < m - 1)
    def _():
        for k in range(n - 1, -1, -1):
            folds[k].start()

    sends = []
    for k in range(n - 1, -1, -1):
        spot = pl.ds(peers[k] * sh, sh)

        @pl.when(w > 0)
        def _():
            folds[k].wait_recv()
            acc[spot] = h[spot] + fold[spot]

        @pl.when(w == 0)
        def _():
            acc[spot] = h[spot]

        if k > 0:
            copy = remote(at(acc, peers[k]), rs.at[k], rs_s.at[k], rs_r.at[k], "lm", peers[k])
            copy.start()
            sends.append(copy)
    here = pl.ds(i * sh, sh)
    total = acc[here]
    for k in range(1, n):
        remote(at(acc, i), rs.at[k], rs_s.at[k], rs_r.at[k], "lm", peers[k]).wait_recv()
        total = total + rs[k]
    value, products = on_shard(here, total)
    full[here] = value
    if products:
        rows = lax.broadcasted_iota(jnp.int32, near.shape[1:], 0)
        tile = jnp.zeros(near.shape[1:], jnp.float32)
        for r, product in enumerate(products):
            tile = jnp.where(rows == r, jnp.sum(jnp.sum(product, axis=0), axis=0, keepdims=True), tile)
        near[i] = tile
        for k in outward:
            copy = remote(near.at[i], near.at[i], near_s.at[k], near_r.at[k], "lm", peers[k])
            copy.start()
            sends.append(copy)
    for k in outward:
        copy = remote(at(full, i), at(full, i), ag_s.at[k], ag_r.at[k], "lm", peers[k])
        copy.start()
        sends.append(copy)
    forwards = [
        remote(at(full, peers[k]), at(full, peers[k], own), fw_s.at[k], fw_r.at[k], "kf", former)
        for k in range(n if pair else 0)
    ]

    def collect(k):
        if k > 0:
            remote(at(full, peers[k]), at(full, peers[k]), ag_s.at[k], ag_r.at[k], "lm", peers[k]).wait_recv()
        if pair:

            @pl.when(w > 0)
            def _():
                forwards[k].start()

    for k in range(n // 2):
        collect(k)
    if products:
        for k in range(1, n):
            remote(near.at[i], near.at[peers[k]], near_s.at[k], near_r.at[k], "lm", peers[k]).wait_recv()
        tile = near[0]
        for j in range(1, n):
            tile = tile + near[j]
        far[w] = tile
        for k in range(1, m):
            copy = remote(far.at[w], far.at[w], far_s.at[k], far_r.at[w], "kf", lax.rem(w + k, m))
            copy.start()
            sends.append(copy)
    for k in range(n // 2, n):
        collect(k)

    def sums():
        for k in range(1, m):
            j = lax.rem(w + k, m)
            remote(far.at[j], far.at[j], far_s.at[k], far_r.at[j], "kf", j).wait_recv()
        tile = far[0]
        for j in range(1, m):
            tile = tile + far[j]
        tile = jnp.sum(tile, axis=1, keepdims=True)
        return [tile[r:r + 1] for r in range(len(products))]

    def finish_pair():
        @pl.when(w < m - 1)
        def _():
            for copy in forwards:
                copy.wait_recv()

        @pl.when(w == m - 1)
        def _():
            full[pl.ds(own, own)] = jnp.zeros((own,) + full.shape[1:], jnp.float32)

    def finish_sends():
        @pl.when(w < m - 1)
        def _():
            for k in range(n):
                folds[k].wait_send()

        for copy in sends:
            copy.wait_send()
        if pair:

            @pl.when(w > 0)
            def _():
                for copy in forwards:
                    copy.wait_send()

    return sums, finish_pair, finish_sends


def columns(g):
    return pl.ds(g * LANES, LANES)


def first_phase(n, m, h, damping, jacobi_scale, res_out, dir_out, scale_out, damp_out, full, fold, acc, rs, near, far, *sems):
    own = acc.shape[0]
    sh = own // n
    state = damping.shape[0]
    i, w = lax.axis_index("lm"), lax.axis_index("kf")
    here, upper = pl.ds(0, own), pl.ds(own, own)
    met = greet(n, m)
    scale, scale_sems = sems[-2], sems[-1]
    rest = pl.ds(state, PAD - state)
    scale[here, rest, :] = jnp.zeros((own, PAD - state, LANES), jnp.float32)
    for g in range(own):
        scale[g, pl.ds(0, state), :] = jacobi_scale[:, columns(g)]
    damp_out[:, rest, :] = jnp.zeros((sh, PAD - state, LANES), jnp.float32)
    for g in range(sh):
        spot = pl.ds(pl.multiple_of((i * sh + g) * LANES, LANES), LANES)
        damp_out[g, pl.ds(0, state), :] = damping[:, spot]
    met()
    scale_copy = remote(
        scale.at[here], scale.at[upper], scale_sems.at[0], scale_sems.at[1], "kf", lax.rem(w + m - 1, m)
    )

    @pl.when(w > 0)
    def _():
        scale_copy.start()

    _, finish_pair, finish_sends = all_reduce(
        n, m, True, h, full, (fold, acc, rs, near, far), sems[:-2], lambda here, total: (-total, ())
    )

    res_out[here] = full[here]
    dir_out[here] = full[here] * scale[here]
    scale_out[here] = scale[here]

    @pl.when(w < m - 1)
    def _():
        scale_copy.wait_recv()

    @pl.when(w == m - 1)
    def _():
        scale[upper] = jnp.zeros((own,) + scale.shape[1:], jnp.float32)

    finish_pair()
    res_out[upper] = full[upper]
    dir_out[upper] = full[upper] * scale[upper]
    scale_out[upper] = scale[upper]

    @pl.when(w > 0)
    def _():
        scale_copy.wait_send()

    finish_sends()


def middle_phase(begun, n, m, h, res, direction, scale, damp, *rest):
    if begun:
        answer_in, *rest = rest
    res_out, dir_out, answer_out, full, fold, acc, rs, near, far, *sems = rest
    own = acc.shape[0]
    here = pl.ds(0, own)
    greet(n, m)()

    def on_shard(here, total):
        along, left, scaled = direction[here], res[here], scale[here]
        applied = total + damp[...] * along
        scaled_applied, scaled_left = scaled * applied, scaled * left
        return applied, (along * applied, left * scaled_applied, applied * scaled_applied, left * scaled_left)

    sums, finish_pair, finish_sends = all_reduce(
        n, m, True, h, full, (fold, acc, rs, near, far), sems, on_shard
    )
    curve, cross, square, energy = sums()
    step = energy / curve
    ratio = (energy - 2.0 * step * cross + step * step * square) / energy

    def advance(part):
        after = res[part] - step * full[part]
        res_out[part] = after
        dir_out[part] = scale[part] * after + ratio * direction[part]

    gained = step * direction[here]
    answer_out[...] = answer_in[...] + gained if begun else gained
    advance(here)
    finish_pair()
    advance(pl.ds(own, own))
    finish_sends()


def last_phase(n, m, h, res, direction, scale, damp, applied_out, step_out, full, fold, acc, rs, near, far, *sems):
    own = acc.shape[0]
    greet(n, m)()

    def on_shard(here, total):
        along, left = direction[here], res[here]
        applied = total + damp[...] * along
        return applied, (along * applied, left * left * scale[here])

    sums, _, finish_sends = all_reduce(
        n, m, False, h, full, (fold, acc, rs, near, far), sems, on_shard
    )
    curve, energy = sums()
    step_out[...] = jnp.broadcast_to(energy / curve, step_out.shape)
    applied_out[...] = full[pl.ds(0, own)]
    finish_sends()


def update_kernel(res, direction, applied, answer_in, step_in, answer_out, res_out):
    own = applied.shape[0]
    state = res_out.shape[0]
    step = step_in[pl.ds(0, 1), pl.ds(0, 1)]
    for g in range(own):
        answer_out[:, columns(g)] = (answer_in[g] + step * direction[g])[:state]
        res_out[:, columns(g)] = (res[g] - step * applied[g])[:state]


def last_update(shape, res, direction, applied, answer, step):
    half = pl.BlockSpec(applied.shape, lambda i: (0, 0, 0))
    whole = pl.BlockSpec(shape, lambda i: (0, 0))
    return pl.pallas_call(
        update_kernel,
        grid=(1,),
        in_specs=[half] * 4 + [pl.BlockSpec(step.shape, lambda i: (0, 0))],
        out_specs=[whole] * 2,
        out_shape=[jax.ShapeDtypeStruct(shape, jnp.float32)] * 2,
        compiler_params=pltpu.CompilerParams(vmem_limit_bytes=LIMIT),
        name="last_update",
    )(res, direction, applied, answer, step)


def phase(kernel, name, number, n, m, outs, extra, *operands):
    pair = operands[0].shape
    own = pair[0] // 2
    tile = pair[1:]
    vmem = pl.BlockSpec(memory_space=pltpu.VMEM)
    dma = pltpu.SemaphoreType.DMA
    return pl.pallas_call(
        functools.partial(kernel, n, m),
        in_specs=[vmem] * len(operands),
        out_specs=[vmem] * len(outs),
        out_shape=[jax.ShapeDtypeStruct(shape, jnp.float32) for shape in outs],
        scratch_shapes=[
            pltpu.VMEM(pair, jnp.float32),
            pltpu.VMEM((own,) + tile, jnp.float32),
            pltpu.VMEM((own,) + tile, jnp.float32),
            pltpu.VMEM((n, own // n) + tile, jnp.float32),
            pltpu.VMEM((n, 8, LANES), jnp.float32),
            pltpu.VMEM((m, 8, LANES), jnp.float32),
        ]
        + [dma((n,))] * 10
        + [dma((m,))] * 2
        + extra,
        compiler_params=pltpu.CompilerParams(collective_id=number, has_side_effects=True, vmem_limit_bytes=LIMIT),
        name=name,
    )(*operands)


def shards(residual_rows, jacobian, nullspace, frame_ids, obs_count, damping, jacobi_scale):
    state, frames = damping.shape
    own = frames // LANES
    blocks = nullspace.shape[0]
    starts = jnp.minimum((frame_ids[:, 0] - lax.axis_index("kf") * frames) >> 7, 2 * own - SPAN)
    n, m = lax.axis_size("lm"), lax.axis_size("kf")
    pair, one, tile = (2 * own, PAD, LANES), (own, PAD, LANES), (8, LANES)
    vmem = pl.BlockSpec(memory_space=pltpu.VMEM)
    gradient, code, inverse, jac, null = local_call(
        gradient_kernel, "local_gradient",
        [
            jax.ShapeDtypeStruct(pair, jnp.float32),
            jax.ShapeDtypeStruct((blocks, LANES), jnp.int32),
            jax.ShapeDtypeStruct((blocks, PICK, LANES), jnp.int32),
            jax.ShapeDtypeStruct((blocks * PAD, LANES), jnp.float32),
            jax.ShapeDtypeStruct(nullspace.shape, nullspace.dtype),
        ],
        [pltpu.VMEM((blocks, LANES), jnp.int32), pltpu.SemaphoreType.DMA((blocks // CHUNK,))],
        [vmem] * 4 + [pl.BlockSpec(memory_space=pltpu.HBM)],
        starts, jnp.transpose(frame_ids), obs_count[None, :], residual_rows,
        jnp.transpose(jacobian, (1, 0, 2)), nullspace,
    )
    jac = jac.reshape(blocks, PAD, LANES)

    def product(field):
        return local_call(
            product_kernel, "local_field", [jax.ShapeDtypeStruct(pair, jnp.float32)], [], [vmem] * 5,
            starts, field, code, inverse, jac, null,
        )[0]

    residual, direction, scale, damp = phase(
        first_phase, "first_phase", 0, n, m, (pair, pair, pair, (own // n, PAD, LANES)),
        [pltpu.VMEM(pair, jnp.float32), pltpu.SemaphoreType.DMA((2,))], gradient, damping, jacobi_scale,
    )
    answer = ()
    for number in range(1, ITERS):
        residual, direction, *answer = phase(
            functools.partial(middle_phase, number > 1), "middle_phase", number, n, m, (pair, pair, one), [],
            product(direction), residual, direction, scale, damp, *answer,
        )
    applied, step = phase(
        last_phase, "last_phase", ITERS, n, m, (one, tile), [], product(direction), residual, direction, scale, damp
    )
    return tuple(last_update(damping.shape, residual, direction, applied, *answer, step))


def solution(mesh):
    placed = (
        P(("lm", "kf"), None),
        P(("lm", "kf"), None, None),
        P(("lm", "kf"), None, None),
        P(("lm", "kf"), None),
        P(("lm", "kf")),
        P(None, "kf"),
        P(None, "kf"),
    )
    return jax.shard_map(
        shards,
        mesh=mesh,
        in_specs=placed,
        out_specs=(P(None, "kf"), P(None, "kf")),
        check_vma=False,
    )
```

```python
import functools

import jax
import jax.numpy as jnp
from jax import lax
from jax.experimental import pallas as pl
from jax.experimental.pallas import tpu as pltpu
from jax.sharding import PartitionSpec as P

ITERS = 2
LANES = 128
PAD = 16
SPAN = 5
CHUNK = 32
PICK = 8
DEAD = 1 << 20
LIMIT = 16 << 20


def spread_over(lifted, factors, first):
    picks = lax.broadcasted_iota(jnp.int32, lifted.shape, 0)
    half = lifted.astype(jnp.bfloat16)
    inner = jnp.zeros(lifted.shape, jnp.float32)
    for i in range(PICK):
        inner = jnp.where(picks == i, jnp.dot(half, factors[first + i], preferred_element_type=jnp.float32), inner)
    half = inner.astype(jnp.bfloat16)
    spread = jnp.zeros(lifted.shape, jnp.float32)
    for i in range(PICK):
        spread = jnp.where(
            picks == i,
            lax.dot_general(
                half, factors[first + i], (((1,), (1,)), ((), ())), preferred_element_type=jnp.float32
            ),
            spread,
        )
    return spread


def sums_of_eight(tiles):
    rows = lax.broadcasted_iota(jnp.int32, tiles[0].shape, 0)
    width = 1
    while width < PICK:
        low = (rows & width) == 0
        tiles = [
            jnp.where(low, left, right) + pltpu.roll(jnp.where(low, right, left), width, axis=0)
            for left, right in zip(tiles[::2], tiles[1::2])
        ]
        width *= 2
    return tiles[0]


def along_lanes(tile, lanes):
    return jnp.take_along_axis(tile, lanes, axis=1, mode="promise_in_bounds")


def scatter_terms(starts, block, i, jac, row_ref, inv_ref, out_ref, even):
    terms = jac * row_ref[pl.ds(i, 1), :]
    terms = jnp.where(even, terms + pltpu.roll(terms, LANES - 1, axis=1), 0.0)
    begin = starts[block]
    for q in range(SPAN):
        lanes = jnp.broadcast_to(inv_ref[i, pl.ds(q, 1), :], terms.shape)
        out_ref[begin + q] += along_lanes(terms, lanes)


def even_lanes():
    return (lax.broadcasted_iota(jnp.int32, (PAD, LANES), 1) & 1) == 0


def product_kernel(starts, field_ref, code_ref, inv_ref, jac_ref, null_ref, out_ref, row_ref):
    out_ref[...] = jnp.zeros_like(out_ref)
    even = even_lanes()

    @pl.loop(0, null_ref.shape[0] // CHUNK)
    def _(step):
        base = pl.multiple_of(step * CHUNK, CHUNK)
        mine = pl.ds(base, CHUNK)
        codes, invs, jacs, factors = code_ref.at[mine], inv_ref.at[mine], jac_ref.at[mine], null_ref.at[mine]
        for first in range(0, CHUNK, PICK):
            tiles = []
            for i in range(first, first + PICK):
                begin = starts[base + i]
                code = jnp.broadcast_to(codes[pl.ds(i, 1), :], (PAD, LANES))
                lanes, part = code & (LANES - 1), code >> 7
                gathered = jnp.zeros((PAD, LANES), jnp.float32)
                for q in range(SPAN):
                    gathered = jnp.where(part == q, along_lanes(field_ref[begin + q], lanes), gathered)
                gathered = gathered * jacs[i]
                tiles.append(gathered[:PICK] + gathered[PICK:])
            row_ref[pl.ds(first, PICK), :] = spread_over(sums_of_eight(tiles), factors, first)
        for i in range(CHUNK):
            scatter_terms(starts, base + i, i, jacs[i], row_ref, invs, out_ref, even)


def gradient_kernel(
    starts, offs_ref, rows_ref, jac_in, null_ref, out_ref, code_ref, inv_ref, jac_ref, row_ref, slot_ref
):
    blocks = null_ref.shape[0]
    chunks = blocks // CHUNK
    out_ref[...] = jnp.zeros_like(out_ref)
    offs = offs_ref[...]
    offs = jnp.transpose(jnp.concatenate([offs] * (LANES // offs.shape[0]), axis=0))
    slot_ref[...] = offs
    lanes = lax.broadcasted_iota(jnp.int32, offs.shape, 1)
    code_ref[...] = along_lanes(offs, lanes >> 1)
    state = jac_in.shape[0]
    for c in range(PAD):
        for g in range(blocks // PICK):
            spot = pl.ds(g * PICK * PAD + c, PICK, stride=PAD)
            if c < state:
                jac_ref[spot, :] = jac_in[c, pl.ds(g * PICK, PICK), :].astype(jnp.float32)
            else:
                jac_ref[spot, :] = jnp.zeros((PICK, LANES), jnp.float32)
    even = even_lanes()
    tile = (PICK, LANES)
    target = lax.broadcasted_iota(jnp.int32, tile, 0) * LANES + lax.broadcasted_iota(jnp.int32, tile, 1)
    @pl.loop(0, chunks)
    def _(step):
        base = pl.multiple_of(step * CHUNK, CHUNK)
        mine = pl.ds(base, CHUNK)
        codes, invs, factors = code_ref.at[mine], inv_ref.at[mine], null_ref.at[mine]
        offsets = slot_ref.at[mine]
        jacs = jac_ref.at[pl.ds(pl.multiple_of(step * CHUNK * PAD, CHUNK * PAD), CHUNK * PAD)]
        residuals = rows_ref[mine, :].astype(jnp.float32)
        lifted = jnp.where(codes[...] < DEAD, residuals, 0.0)
        for first in range(0, CHUNK, PICK):
            row_ref[pl.ds(first, PICK), :] = spread_over(lifted[first:first + PICK], factors, first)
        for i in range(CHUNK):
            offset = jnp.broadcast_to(offsets[pl.ds(i, 1), :], tile)
            at = jnp.zeros(tile, jnp.int32)
            width = offs_ref.shape[0] // 2
            while width > 0:
                at = jnp.where(along_lanes(offset, at + width) <= target, at + width, at)
                width //= 2
            invs[i] = jnp.where(along_lanes(offset, at) == target, 2 * at, LANES - 1)
        for i in range(CHUNK):
            scatter_terms(starts, base + i, i, jacs[pl.ds(i * PAD, PAD), :], row_ref, invs, out_ref, even)


def local_call(kernel, name, outs, extra, in_specs, *operands):
    vmem = pl.BlockSpec(memory_space=pltpu.VMEM)
    return pl.pallas_call(
        kernel,
        in_specs=[pl.BlockSpec(memory_space=pltpu.SMEM)] + in_specs,
        out_specs=[vmem] * len(outs),
        out_shape=outs,
        scratch_shapes=[pltpu.VMEM((CHUNK, LANES), jnp.float32)] + extra,
        compiler_params=pltpu.CompilerParams(vmem_limit_bytes=LIMIT),
        name=name,
    )(*operands)


def remote(src, dst, send, recv, axis, index):
    where = dict(zip(axis, index)) if isinstance(axis, tuple) else {axis: index}
    return pltpu.make_async_remote_copy(
        src_ref=src, dst_ref=dst, send_sem=send, recv_sem=recv,
        device_id=where, device_id_type=pl.DeviceIdType.MESH,
    )


def partner(i, k):
    bit, flipped = 1, i * 0
    while bit <= k or bit == 1:
        digit = lax.rem(i // bit, 2)
        flipped = flipped + bit * ((1 - 2 * digit) if k & bit else 0)
        bit *= 2
    return i + flipped


def greet(n, m):
    i, w = lax.axis_index("lm"), lax.axis_index("kf")
    barrier = pltpu.get_barrier_semaphore()
    count = 0

    def signal(j, v):
        pl.semaphore_signal(barrier, inc=1, device_id={"lm": j, "kf": v}, device_id_type=pl.DeviceIdType.MESH)
        return 1

    for k in range(n - 1, -1, -1):
        for step in (1, m - 1):
            count += signal(partner(i, k), lax.rem(w + step, m))
        if k > 0:
            count += signal(partner(i, k), w)
    for step in range(2, m - 1):
        count += signal(i, lax.rem(w + step, m))
    return lambda: pl.semaphore_wait(barrier, count)


def all_reduce(n, m, pair, h, full, bufs, sems, on_shard):
    acc, rs, near, far = bufs
    up_s, up_r, rs_s, rs_r, ag_s, ag_r, fw_s, fw_r, near_s, near_r, far_s, far_r = sems
    own = h.shape[0] // 2
    sh = own // n
    i, w = lax.axis_index("lm"), lax.axis_index("kf")
    later, former = lax.rem(w + 1, m), lax.rem(w + m - 1, m)

    def at(ref, j, base=0):
        return ref.at[pl.ds(base + j * sh, sh)]

    peers = [partner(i, k) for k in range(n)]
    outward = range(n - 1, 0, -1)
    uppers = [
        remote(at(h, peers[k], own), rs.at[n + k], up_s.at[k], up_r.at[k], ("lm", "kf"), (peers[k], later))
        for k in range(n)
    ]
    lowers = [
        remote(at(h, peers[k]), rs.at[k], rs_s.at[k], rs_r.at[k], "lm", peers[k]) for k in outward
    ]
    for k in range(n - 1, -1, -1):

        @pl.when(w < m - 1)
        def _():
            uppers[k].start()

        if k > 0:
            lowers[n - 1 - k].start()
    sends = list(lowers)
    here = pl.ds(i * sh, sh)
    total = h[here]
    for copy, k in zip(lowers[::-1], range(1, n)):
        copy.wait_recv()
        total = total + rs[k]
    acc[...] = total

    @pl.when(w > 0)
    def _():
        more = acc[...]
        for k in range(n):
            uppers[k].wait_recv()
            more = more + rs[n + k]
        acc[...] = more

    total = acc[...]
    value, products = on_shard(here, total)
    full[here] = value
    if products:
        rows = lax.broadcasted_iota(jnp.int32, near.shape[1:], 0)
        tile = jnp.zeros(near.shape[1:], jnp.float32)
        for r, product in enumerate(products):
            tile = jnp.where(rows == r, jnp.sum(jnp.sum(product, axis=0), axis=0, keepdims=True), tile)
        near[i] = tile
        for k in outward:
            copy = remote(near.at[i], near.at[i], near_s.at[k], near_r.at[k], "lm", peers[k])
            copy.start()
            sends.append(copy)
    for k in outward:
        copy = remote(at(full, i), at(full, i), ag_s.at[k], ag_r.at[k], "lm", peers[k])
        copy.start()
        sends.append(copy)
    forwards = [
        remote(at(full, peers[k]), at(full, peers[k], own), fw_s.at[k], fw_r.at[k], "kf", former)
        for k in range(n if pair else 0)
    ]

    def collect(k):
        if k > 0:
            remote(at(full, peers[k]), at(full, peers[k]), ag_s.at[k], ag_r.at[k], "lm", peers[k]).wait_recv()
        if pair:

            @pl.when(w > 0)
            def _():
                forwards[k].start()

    for k in range(n // 2):
        collect(k)
    if products:
        for k in range(1, n):
            remote(near.at[i], near.at[peers[k]], near_s.at[k], near_r.at[k], "lm", peers[k]).wait_recv()
        tile = near[0]
        for j in range(1, n):
            tile = tile + near[j]
        far[w] = tile
        for k in range(1, m):
            copy = remote(far.at[w], far.at[w], far_s.at[k], far_r.at[w], "kf", lax.rem(w + k, m))
            copy.start()
            sends.append(copy)
    for k in range(n // 2, n):
        collect(k)

    def sums():
        for k in range(1, m):
            j = lax.rem(w + k, m)
            remote(far.at[j], far.at[j], far_s.at[k], far_r.at[j], "kf", j).wait_recv()
        tile = far[0]
        for j in range(1, m):
            tile = tile + far[j]
        tile = jnp.sum(tile, axis=1, keepdims=True)
        return [tile[r:r + 1] for r in range(len(products))]

    def finish_pair():
        @pl.when(w < m - 1)
        def _():
            for copy in forwards:
                copy.wait_recv()

        @pl.when(w == m - 1)
        def _():
            full[pl.ds(own, own)] = jnp.zeros((own,) + full.shape[1:], jnp.float32)

    def finish_sends():
        @pl.when(w < m - 1)
        def _():
            for k in range(n):
                uppers[k].wait_send()

        for copy in sends:
            copy.wait_send()
        if pair:

            @pl.when(w > 0)
            def _():
                for copy in forwards:
                    copy.wait_send()

    return sums, finish_pair, finish_sends


def columns(g):
    return pl.ds(g * LANES, LANES)


def first_phase(n, m, h, damping, jacobi_scale, res_out, dir_out, scale_out, damp_out, full, acc, rs, near, far, *sems):
    own = full.shape[0] // 2
    sh = own // n
    state = damping.shape[0]
    i, w = lax.axis_index("lm"), lax.axis_index("kf")
    here, upper = pl.ds(0, own), pl.ds(own, own)
    met = greet(n, m)
    scale, scale_sems = sems[-2], sems[-1]
    rest = pl.ds(state, PAD - state)
    scale[here, rest, :] = jnp.zeros((own, PAD - state, LANES), jnp.float32)
    for g in range(own):
        scale[g, pl.ds(0, state), :] = jacobi_scale[:, columns(g)]
    damp_out[:, rest, :] = jnp.zeros((sh, PAD - state, LANES), jnp.float32)
    for g in range(sh):
        spot = pl.ds(pl.multiple_of((i * sh + g) * LANES, LANES), LANES)
        damp_out[g, pl.ds(0, state), :] = damping[:, spot]
    met()
    scale_copy = remote(
        scale.at[here], scale.at[upper], scale_sems.at[0], scale_sems.at[1], "kf", lax.rem(w + m - 1, m)
    )

    @pl.when(w > 0)
    def _():
        scale_copy.start()

    _, finish_pair, finish_sends = all_reduce(
        n, m, True, h, full, (acc, rs, near, far), sems[:-2], lambda here, total: (-total, ())
    )

    res_out[here] = full[here]
    dir_out[here] = full[here] * scale[here]
    scale_out[here] = scale[here]

    @pl.when(w < m - 1)
    def _():
        scale_copy.wait_recv()

    @pl.when(w == m - 1)
    def _():
        scale[upper] = jnp.zeros((own,) + scale.shape[1:], jnp.float32)

    finish_pair()
    res_out[upper] = full[upper]
    dir_out[upper] = full[upper] * scale[upper]
    scale_out[upper] = scale[upper]

    @pl.when(w > 0)
    def _():
        scale_copy.wait_send()

    finish_sends()


def middle_phase(begun, n, m, h, res, direction, scale, damp, *rest):
    if begun:
        answer_in, *rest = rest
    res_out, dir_out, answer_out, full, acc, rs, near, far, *sems = rest
    own = full.shape[0] // 2
    here = pl.ds(0, own)
    greet(n, m)()

    def on_shard(here, total):
        along, left, scaled = direction[here], res[here], scale[here]
        applied = total + damp[...] * along
        scaled_applied, scaled_left = scaled * applied, scaled * left
        return applied, (along * applied, left * scaled_applied, applied * scaled_applied, left * scaled_left)

    sums, finish_pair, finish_sends = all_reduce(
        n, m, True, h, full, (acc, rs, near, far), sems, on_shard
    )
    curve, cross, square, energy = sums()
    step = energy / curve
    ratio = (energy - 2.0 * step * cross + step * step * square) / energy

    def advance(part):
        after = res[part] - step * full[part]
        res_out[part] = after
        dir_out[part] = scale[part] * after + ratio * direction[part]

    gained = step * direction[here]
    answer_out[...] = answer_in[...] + gained if begun else gained
    advance(here)
    finish_pair()
    advance(pl.ds(own, own))
    finish_sends()


def last_phase(n, m, h, res, direction, scale, damp, applied_out, step_out, full, acc, rs, near, far, *sems):
    own = full.shape[0] // 2
    greet(n, m)()

    def on_shard(here, total):
        along, left = direction[here], res[here]
        applied = total + damp[...] * along
        return applied, (along * applied, left * left * scale[here])

    sums, _, finish_sends = all_reduce(
        n, m, False, h, full, (acc, rs, near, far), sems, on_shard
    )
    curve, energy = sums()
    step_out[...] = jnp.broadcast_to(energy / curve, step_out.shape)
    applied_out[...] = full[pl.ds(0, own)]
    finish_sends()


def update_kernel(res, direction, applied, answer_in, step_in, answer_out, res_out):
    own = applied.shape[0]
    state = res_out.shape[0]
    step = step_in[pl.ds(0, 1), pl.ds(0, 1)]
    for g in range(own):
        answer_out[:, columns(g)] = (answer_in[g] + step * direction[g])[:state]
        res_out[:, columns(g)] = (res[g] - step * applied[g])[:state]


def last_update(shape, res, direction, applied, answer, step):
    half = pl.BlockSpec(applied.shape, lambda i: (0, 0, 0))
    whole = pl.BlockSpec(shape, lambda i: (0, 0))
    return pl.pallas_call(
        update_kernel,
        grid=(1,),
        in_specs=[half] * 4 + [pl.BlockSpec(step.shape, lambda i: (0, 0))],
        out_specs=[whole] * 2,
        out_shape=[jax.ShapeDtypeStruct(shape, jnp.float32)] * 2,
        compiler_params=pltpu.CompilerParams(vmem_limit_bytes=LIMIT),
        name="last_update",
    )(res, direction, applied, answer, step)


def phase(kernel, name, number, n, m, outs, extra, *operands):
    pair = operands[0].shape
    own = pair[0] // 2
    tile = pair[1:]
    vmem = pl.BlockSpec(memory_space=pltpu.VMEM)
    dma = pltpu.SemaphoreType.DMA
    return pl.pallas_call(
        functools.partial(kernel, n, m),
        in_specs=[vmem] * len(operands),
        out_specs=[vmem] * len(outs),
        out_shape=[jax.ShapeDtypeStruct(shape, jnp.float32) for shape in outs],
        scratch_shapes=[
            pltpu.VMEM(pair, jnp.float32),
            pltpu.VMEM((own // n,) + tile, jnp.float32),
            pltpu.VMEM((2 * n, own // n) + tile, jnp.float32),
            pltpu.VMEM((n, 8, LANES), jnp.float32),
            pltpu.VMEM((m, 8, LANES), jnp.float32),
        ]
        + [dma((n,))] * 10
        + [dma((m,))] * 2
        + extra,
        compiler_params=pltpu.CompilerParams(collective_id=number, has_side_effects=True, vmem_limit_bytes=LIMIT),
        name=name,
    )(*operands)


def shards(residual_rows, jacobian, nullspace, frame_ids, obs_count, damping, jacobi_scale):
    state, frames = damping.shape
    own = frames // LANES
    blocks = nullspace.shape[0]
    ids = jnp.transpose(frame_ids) - lax.axis_index("kf") * frames
    starts = jnp.minimum(ids[0] >> 7, 2 * own - SPAN)
    slots = lax.broadcasted_iota(jnp.int32, ids.shape, 0)
    offsets = jnp.where(slots < obs_count[None, :], ids - starts[None, :] * LANES, DEAD)
    n, m = lax.axis_size("lm"), lax.axis_size("kf")
    pair, one, tile = (2 * own, PAD, LANES), (own, PAD, LANES), (8, LANES)
    vmem = pl.BlockSpec(memory_space=pltpu.VMEM)
    gradient, code, inverse, jac = local_call(
        gradient_kernel, "local_gradient",
        [
            jax.ShapeDtypeStruct(pair, jnp.float32),
            jax.ShapeDtypeStruct((blocks, LANES), jnp.int32),
            jax.ShapeDtypeStruct((blocks, PICK, LANES), jnp.int32),
            jax.ShapeDtypeStruct((blocks * PAD, LANES), jnp.float32),
        ],
        [pltpu.VMEM((blocks, LANES), jnp.int32)], [vmem] * 4,
        starts, offsets, residual_rows, jnp.transpose(jacobian, (1, 0, 2)), nullspace,
    )
    jac = jac.reshape(blocks, PAD, LANES)

    def product(field):
        return local_call(
            product_kernel, "local_field", [jax.ShapeDtypeStruct(pair, jnp.float32)], [], [vmem] * 5,
            starts, field, code, inverse, jac, nullspace,
        )[0]

    residual, direction, scale, damp = phase(
        first_phase, "first_phase", 0, n, m, (pair, pair, pair, (own // n, PAD, LANES)),
        [pltpu.VMEM(pair, jnp.float32), pltpu.SemaphoreType.DMA((2,))], gradient, damping, jacobi_scale,
    )
    answer = ()
    for number in range(1, ITERS):
        residual, direction, *answer = phase(
            functools.partial(middle_phase, number > 1), "middle_phase", number, n, m, (pair, pair, one), [],
            product(direction), residual, direction, scale, damp, *answer,
        )
    applied, step = phase(
        last_phase, "last_phase", ITERS, n, m, (one, tile), [], product(direction), residual, direction, scale, damp
    )
    return tuple(last_update(damping.shape, residual, direction, applied, *answer, step))


def solution(mesh):
    placed = (
        P(("lm", "kf"), None),
        P(("lm", "kf"), None, None),
        P(("lm", "kf"), None, None),
        P(("lm", "kf"), None),
        P(("lm", "kf")),
        P(None, "kf"),
        P(None, "kf"),
    )
    return jax.shard_map(
        shards,
        mesh=mesh,
        in_specs=placed,
        out_specs=(P(None, "kf"), P(None, "kf")),
        check_vma=False,
    )
```

```python
import functools

import jax
import jax.numpy as jnp
from jax import lax
from jax.experimental import pallas as pl
from jax.experimental.pallas import tpu as pltpu
from jax.sharding import PartitionSpec as P

ITERS = 2
LANES = 128
PAD = 16
SPAN = 5
CHUNK = 32
PICK = 8
DEAD = 1 << 20
LIMIT = 16 << 20


def spread_over(lifted, factors, first):
    picks = lax.broadcasted_iota(jnp.int32, lifted.shape, 0)
    half = lifted.astype(jnp.bfloat16)
    inner = jnp.zeros(lifted.shape, jnp.float32)
    for i in range(PICK):
        inner = jnp.where(picks == i, jnp.dot(half, factors[first + i], preferred_element_type=jnp.float32), inner)
    half = inner.astype(jnp.bfloat16)
    spread = jnp.zeros(lifted.shape, jnp.float32)
    for i in range(PICK):
        spread = jnp.where(
            picks == i,
            lax.dot_general(
                half, factors[first + i], (((1,), (1,)), ((), ())), preferred_element_type=jnp.float32
            ),
            spread,
        )
    return spread


def sums_of_eight(tiles):
    rows = lax.broadcasted_iota(jnp.int32, tiles[0].shape, 0)
    width = 1
    while width < PICK:
        low = (rows & width) == 0
        tiles = [
            jnp.where(low, left, right) + pltpu.roll(jnp.where(low, right, left), width, axis=0)
            for left, right in zip(tiles[::2], tiles[1::2])
        ]
        width *= 2
    return tiles[0]


def along_lanes(tile, lanes):
    dims = lax.GatherDimensionNumbers(
        offset_dims=(), collapsed_slice_dims=(1,), start_index_map=(1,),
        operand_batching_dims=(0,), start_indices_batching_dims=(0,),
    )
    return lax.gather(
        tile, lanes[..., None], dims, slice_sizes=(1, 1), mode=lax.GatherScatterMode.PROMISE_IN_BOUNDS
    )


def scatter_terms(starts, block, i, jac, row_ref, inv_ref, out_ref, even):
    terms = jac * row_ref[pl.ds(i, 1), :]
    terms = jnp.where(even, terms + pltpu.roll(terms, LANES - 1, axis=1), 0.0)
    begin = starts[block]
    for q in range(SPAN):
        lanes = jnp.broadcast_to(inv_ref[i, pl.ds(q, 1), :], terms.shape)
        out_ref[begin + q] += along_lanes(terms, lanes)


def even_lanes():
    return (lax.broadcasted_iota(jnp.int32, (PAD, LANES), 1) & 1) == 0


def product_kernel(starts, field_ref, code_ref, inv_ref, jac_ref, null_ref, out_ref, row_ref):
    out_ref[...] = jnp.zeros_like(out_ref)
    even = even_lanes()

    @pl.loop(0, null_ref.shape[0] // CHUNK)
    def _(step):
        base = pl.multiple_of(step * CHUNK, CHUNK)
        mine = pl.ds(base, CHUNK)
        codes, invs, jacs, factors = code_ref.at[mine], inv_ref.at[mine], jac_ref.at[mine], null_ref.at[mine]
        for first in range(0, CHUNK, PICK):
            tiles = []
            for i in range(first, first + PICK):
                begin = starts[base + i]
                code = jnp.broadcast_to(codes[pl.ds(i, 1), :], (PAD, LANES))
                lanes, part = code & (LANES - 1), code >> 7
                gathered = jnp.zeros((PAD, LANES), jnp.float32)
                for q in range(SPAN):
                    gathered = jnp.where(part == q, along_lanes(field_ref[begin + q], lanes), gathered)
                gathered = gathered * jacs[i]
                tiles.append(gathered[:PICK] + gathered[PICK:])
            row_ref[pl.ds(first, PICK), :] = spread_over(sums_of_eight(tiles), factors, first)
        for i in range(CHUNK):
            scatter_terms(starts, base + i, i, jacs[i], row_ref, invs, out_ref, even)


def gradient_kernel(
    starts, offs_ref, rows_ref, jac_in, null_ref, out_ref, code_ref, inv_ref, jac_ref, row_ref, slot_ref
):
    blocks = null_ref.shape[0]
    chunks = blocks // CHUNK
    out_ref[...] = jnp.zeros_like(out_ref)
    offs = offs_ref[...]
    offs = jnp.transpose(jnp.concatenate([offs] * (LANES // offs.shape[0]), axis=0))
    slot_ref[...] = offs
    lanes = lax.broadcasted_iota(jnp.int32, offs.shape, 1)
    code_ref[...] = along_lanes(offs, lanes >> 1)
    state = jac_in.shape[0]
    for c in range(PAD):
        for g in range(blocks // PICK):
            spot = pl.ds(g * PICK * PAD + c, PICK, stride=PAD)
            if c < state:
                jac_ref[spot, :] = jac_in[c, pl.ds(g * PICK, PICK), :].astype(jnp.float32)
            else:
                jac_ref[spot, :] = jnp.zeros((PICK, LANES), jnp.float32)
    even = even_lanes()
    tile = (PICK, LANES)
    target = lax.broadcasted_iota(jnp.int32, tile, 0) * LANES + lax.broadcasted_iota(jnp.int32, tile, 1)
    @pl.loop(0, chunks)
    def _(step):
        base = pl.multiple_of(step * CHUNK, CHUNK)
        mine = pl.ds(base, CHUNK)
        codes, invs, factors = code_ref.at[mine], inv_ref.at[mine], null_ref.at[mine]
        offsets = slot_ref.at[mine]
        jacs = jac_ref.at[pl.ds(pl.multiple_of(step * CHUNK * PAD, CHUNK * PAD), CHUNK * PAD)]
        residuals = rows_ref[mine, :].astype(jnp.float32)
        lifted = jnp.where(codes[...] < DEAD, residuals, 0.0)
        for first in range(0, CHUNK, PICK):
            row_ref[pl.ds(first, PICK), :] = spread_over(lifted[first:first + PICK], factors, first)
        for i in range(CHUNK):
            offset = jnp.broadcast_to(offsets[pl.ds(i, 1), :], tile)
            at = jnp.zeros(tile, jnp.int32)
            width = offs_ref.shape[0] // 2
            while width > 0:
                at = jnp.where(along_lanes(offset, at + width) <= target, at + width, at)
                width //= 2
            invs[i] = jnp.where(along_lanes(offset, at) == target, 2 * at, LANES - 1)
        for i in range(CHUNK):
            scatter_terms(starts, base + i, i, jacs[pl.ds(i * PAD, PAD), :], row_ref, invs, out_ref, even)


def local_call(kernel, name, outs, extra, in_specs, *operands):
    vmem = pl.BlockSpec(memory_space=pltpu.VMEM)
    return pl.pallas_call(
        kernel,
        in_specs=[pl.BlockSpec(memory_space=pltpu.SMEM)] + in_specs,
        out_specs=[vmem] * len(outs),
        out_shape=outs,
        scratch_shapes=[pltpu.VMEM((CHUNK, LANES), jnp.float32)] + extra,
        compiler_params=pltpu.CompilerParams(vmem_limit_bytes=LIMIT),
        name=name,
    )(*operands)


def remote(src, dst, send, recv, axis, index):
    return pltpu.make_async_remote_copy(
        src_ref=src, dst_ref=dst, send_sem=send, recv_sem=recv,
        device_id={axis: index}, device_id_type=pl.DeviceIdType.MESH,
    )


def partner(i, k):
    bit, flipped = 1, i * 0
    while bit <= k or bit == 1:
        digit = lax.rem(i // bit, 2)
        flipped = flipped + bit * ((1 - 2 * digit) if k & bit else 0)
        bit *= 2
    return i + flipped


def greet(n, m):
    i, w = lax.axis_index("lm"), lax.axis_index("kf")
    barrier = pltpu.get_barrier_semaphore()
    for k in range(n - 1, 0, -1):
        pl.semaphore_signal(
            barrier, inc=1, device_id={"lm": partner(i, k)}, device_id_type=pl.DeviceIdType.MESH
        )
    for k in range(1, m):
        pl.semaphore_signal(
            barrier, inc=1, device_id={"kf": lax.rem(w + k, m)}, device_id_type=pl.DeviceIdType.MESH
        )
    return lambda: pl.semaphore_wait(barrier, n - 1 + m - 1)


def all_reduce(n, m, pair, h, full, bufs, sems, on_shard):
    fold, acc, rs, near, far = bufs
    fold_s, fold_r, rs_s, rs_r, ag_s, ag_r, fw_s, fw_r, near_s, near_r, far_s, far_r = sems
    own = acc.shape[0]
    sh = own // n
    i, w = lax.axis_index("lm"), lax.axis_index("kf")
    later, former = lax.rem(w + 1, m), lax.rem(w + m - 1, m)

    def at(ref, j, base=0):
        return ref.at[pl.ds(base + j * sh, sh)]

    peers = [partner(i, k) for k in range(n)]
    outward = range(n - 1, 0, -1)
    folds = {
        k: remote(at(h, peers[k], own), at(fold, peers[k]), fold_s.at[k], fold_r.at[k], "kf", later) for k in range(n)
    }

    @pl.when(w < m - 1)
    def _():
        for k in range(n - 1, -1, -1):
            folds[k].start()

    sends = []
    for k in range(n - 1, -1, -1):
        spot = pl.ds(peers[k] * sh, sh)

        @pl.when(w > 0)
        def _():
            folds[k].wait_recv()
            acc[spot] = h[spot] + fold[spot]

        @pl.when(w == 0)
        def _():
            acc[spot] = h[spot]

        if k > 0:
            copy = remote(at(acc, peers[k]), rs.at[k], rs_s.at[k], rs_r.at[k], "lm", peers[k])
            copy.start()
            sends.append(copy)
    here = pl.ds(i * sh, sh)
    total = acc[here]
    for k in range(1, n):
        remote(at(acc, i), rs.at[k], rs_s.at[k], rs_r.at[k], "lm", peers[k]).wait_recv()
        total = total + rs[k]
    value, products = on_shard(here, total)
    full[here] = value
    if products:
        rows = lax.broadcasted_iota(jnp.int32, near.shape[1:], 0)
        tile = jnp.zeros(near.shape[1:], jnp.float32)
        for r, product in enumerate(products):
            tile = jnp.where(rows == r, jnp.sum(jnp.sum(product, axis=0), axis=0, keepdims=True), tile)
        near[i] = tile
        for k in outward:
            copy = remote(near.at[i], near.at[i], near_s.at[k], near_r.at[k], "lm", peers[k])
            copy.start()
            sends.append(copy)
    for k in outward:
        copy = remote(at(full, i), at(full, i), ag_s.at[k], ag_r.at[k], "lm", peers[k])
        copy.start()
        sends.append(copy)
    forwards = [
        remote(at(full, peers[k]), at(full, peers[k], own), fw_s.at[k], fw_r.at[k], "kf", former)
        for k in range(n if pair else 0)
    ]

    def collect(k):
        if k > 0:
            remote(at(full, peers[k]), at(full, peers[k]), ag_s.at[k], ag_r.at[k], "lm", peers[k]).wait_recv()
        if pair:

            @pl.when(w > 0)
            def _():
                forwards[k].start()

    for k in range(n // 2):
        collect(k)
    if products:
        for k in range(1, n):
            remote(near.at[i], near.at[peers[k]], near_s.at[k], near_r.at[k], "lm", peers[k]).wait_recv()
        tile = near[0]
        for j in range(1, n):
            tile = tile + near[j]
        far[w] = tile
        for k in range(1, m):
            copy = remote(far.at[w], far.at[w], far_s.at[k], far_r.at[w], "kf", lax.rem(w + k, m))
            copy.start()
            sends.append(copy)
    for k in range(n // 2, n):
        collect(k)

    def sums():
        for k in range(1, m):
            j = lax.rem(w + k, m)
            remote(far.at[j], far.at[j], far_s.at[k], far_r.at[j], "kf", j).wait_recv()
        tile = far[0]
        for j in range(1, m):
            tile = tile + far[j]
        tile = jnp.sum(tile, axis=1, keepdims=True)
        return [tile[r:r + 1] for r in range(len(products))]

    def finish_pair():
        @pl.when(w < m - 1)
        def _():
            for copy in forwards:
                copy.wait_recv()

        @pl.when(w == m - 1)
        def _():
            full[pl.ds(own, own)] = jnp.zeros((own,) + full.shape[1:], jnp.float32)

    def finish_sends():
        @pl.when(w < m - 1)
        def _():
            for k in range(n):
                folds[k].wait_send()

        for copy in sends:
            copy.wait_send()
        if pair:

            @pl.when(w > 0)
            def _():
                for copy in forwards:
                    copy.wait_send()

    return sums, finish_pair, finish_sends


def columns(g):
    return pl.ds(g * LANES, LANES)


def first_phase(n, m, h, damping, jacobi_scale, res_out, dir_out, scale_out, damp_out, full, fold, acc, rs, near, far, *sems):
    own = acc.shape[0]
    sh = own // n
    state = damping.shape[0]
    i, w = lax.axis_index("lm"), lax.axis_index("kf")
    here, upper = pl.ds(0, own), pl.ds(own, own)
    met = greet(n, m)
    scale, scale_sems = sems[-2], sems[-1]
    rest = pl.ds(state, PAD - state)
    scale[here, rest, :] = jnp.zeros((own, PAD - state, LANES), jnp.float32)
    for g in range(own):
        scale[g, pl.ds(0, state), :] = jacobi_scale[:, columns(g)]
    damp_out[:, rest, :] = jnp.zeros((sh, PAD - state, LANES), jnp.float32)
    for g in range(sh):
        spot = pl.ds(pl.multiple_of((i * sh + g) * LANES, LANES), LANES)
        damp_out[g, pl.ds(0, state), :] = damping[:, spot]
    met()
    scale_copy = remote(
        scale.at[here], scale.at[upper], scale_sems.at[0], scale_sems.at[1], "kf", lax.rem(w + m - 1, m)
    )

    @pl.when(w > 0)
    def _():
        scale_copy.start()

    _, finish_pair, finish_sends = all_reduce(
        n, m, True, h, full, (fold, acc, rs, near, far), sems[:-2], lambda here, total: (-total, ())
    )

    res_out[here] = full[here]
    dir_out[here] = full[here] * scale[here]
    scale_out[here] = scale[here]

    @pl.when(w < m - 1)
    def _():
        scale_copy.wait_recv()

    @pl.when(w == m - 1)
    def _():
        scale[upper] = jnp.zeros((own,) + scale.shape[1:], jnp.float32)

    finish_pair()
    res_out[upper] = full[upper]
    dir_out[upper] = full[upper] * scale[upper]
    scale_out[upper] = scale[upper]

    @pl.when(w > 0)
    def _():
        scale_copy.wait_send()

    finish_sends()


def middle_phase(begun, n, m, h, res, direction, scale, damp, *rest):
    if begun:
        answer_in, *rest = rest
    res_out, dir_out, answer_out, full, fold, acc, rs, near, far, *sems = rest
    own = acc.shape[0]
    here = pl.ds(0, own)
    greet(n, m)()

    def on_shard(here, total):
        along, left, scaled = direction[here], res[here], scale[here]
        applied = total + damp[...] * along
        scaled_applied, scaled_left = scaled * applied, scaled * left
        return applied, (along * applied, left * scaled_applied, applied * scaled_applied, left * scaled_left)

    sums, finish_pair, finish_sends = all_reduce(
        n, m, True, h, full, (fold, acc, rs, near, far), sems, on_shard
    )
    curve, cross, square, energy = sums()
    step = energy / curve
    ratio = (energy - 2.0 * step * cross + step * step * square) / energy

    def advance(part):
        after = res[part] - step * full[part]
        res_out[part] = after
        dir_out[part] = scale[part] * after + ratio * direction[part]

    gained = step * direction[here]
    answer_out[...] = answer_in[...] + gained if begun else gained
    advance(here)
    finish_pair()
    advance(pl.ds(own, own))
    finish_sends()


def last_phase(n, m, h, res, direction, scale, damp, applied_out, step_out, full, fold, acc, rs, near, far, *sems):
    own = acc.shape[0]
    greet(n, m)()

    def on_shard(here, total):
        along, left = direction[here], res[here]
        applied = total + damp[...] * along
        return applied, (along * applied, left * left * scale[here])

    sums, _, finish_sends = all_reduce(
        n, m, False, h, full, (fold, acc, rs, near, far), sems, on_shard
    )
    curve, energy = sums()
    step_out[...] = jnp.broadcast_to(energy / curve, step_out.shape)
    applied_out[...] = full[pl.ds(0, own)]
    finish_sends()


def update_kernel(res, direction, applied, answer_in, step_in, answer_out, res_out):
    own = applied.shape[0]
    state = res_out.shape[0]
    step = step_in[pl.ds(0, 1), pl.ds(0, 1)]
    for g in range(own):
        answer_out[:, columns(g)] = (answer_in[g] + step * direction[g])[:state]
        res_out[:, columns(g)] = (res[g] - step * applied[g])[:state]


def last_update(shape, res, direction, applied, answer, step):
    half = pl.BlockSpec(applied.shape, lambda i: (0, 0, 0))
    whole = pl.BlockSpec(shape, lambda i: (0, 0))
    return pl.pallas_call(
        update_kernel,
        grid=(1,),
        in_specs=[half] * 4 + [pl.BlockSpec(step.shape, lambda i: (0, 0))],
        out_specs=[whole] * 2,
        out_shape=[jax.ShapeDtypeStruct(shape, jnp.float32)] * 2,
        compiler_params=pltpu.CompilerParams(vmem_limit_bytes=LIMIT),
        name="last_update",
    )(res, direction, applied, answer, step)


def phase(kernel, name, number, n, m, outs, extra, *operands):
    pair = operands[0].shape
    own = pair[0] // 2
    tile = pair[1:]
    vmem = pl.BlockSpec(memory_space=pltpu.VMEM)
    dma = pltpu.SemaphoreType.DMA
    return pl.pallas_call(
        functools.partial(kernel, n, m),
        in_specs=[vmem] * len(operands),
        out_specs=[vmem] * len(outs),
        out_shape=[jax.ShapeDtypeStruct(shape, jnp.float32) for shape in outs],
        scratch_shapes=[
            pltpu.VMEM(pair, jnp.float32),
            pltpu.VMEM((own,) + tile, jnp.float32),
            pltpu.VMEM((own,) + tile, jnp.float32),
            pltpu.VMEM((n, own // n) + tile, jnp.float32),
            pltpu.VMEM((n, 8, LANES), jnp.float32),
            pltpu.VMEM((m, 8, LANES), jnp.float32),
        ]
        + [dma((n,))] * 10
        + [dma((m,))] * 2
        + extra,
        compiler_params=pltpu.CompilerParams(collective_id=number, has_side_effects=True, vmem_limit_bytes=LIMIT),
        name=name,
    )(*operands)


def shards(residual_rows, jacobian, nullspace, frame_ids, obs_count, damping, jacobi_scale):
    state, frames = damping.shape
    own = frames // LANES
    blocks = nullspace.shape[0]
    ids = jnp.transpose(frame_ids) - lax.axis_index("kf") * frames
    starts = jnp.minimum(ids[0] >> 7, 2 * own - SPAN)
    slots = lax.broadcasted_iota(jnp.int32, ids.shape, 0)
    offsets = jnp.where(slots < obs_count[None, :], ids - starts[None, :] * LANES, DEAD)
    n, m = lax.axis_size("lm"), lax.axis_size("kf")
    pair, one, tile = (2 * own, PAD, LANES), (own, PAD, LANES), (8, LANES)
    vmem = pl.BlockSpec(memory_space=pltpu.VMEM)
    gradient, code, inverse, jac = local_call(
        gradient_kernel, "local_gradient",
        [
            jax.ShapeDtypeStruct(pair, jnp.float32),
            jax.ShapeDtypeStruct((blocks, LANES), jnp.int32),
            jax.ShapeDtypeStruct((blocks, PICK, LANES), jnp.int32),
            jax.ShapeDtypeStruct((blocks * PAD, LANES), jnp.float32),
        ],
        [pltpu.VMEM((blocks, LANES), jnp.int32)], [vmem] * 4,
        starts, offsets, residual_rows, jnp.transpose(jacobian, (1, 0, 2)), nullspace,
    )
    jac = jac.reshape(blocks, PAD, LANES)

    def product(field):
        return local_call(
            product_kernel, "local_field", [jax.ShapeDtypeStruct(pair, jnp.float32)], [], [vmem] * 5,
            starts, field, code, inverse, jac, nullspace,
        )[0]

    residual, direction, scale, damp = phase(
        first_phase, "first_phase", 0, n, m, (pair, pair, pair, (own // n, PAD, LANES)),
        [pltpu.VMEM(pair, jnp.float32), pltpu.SemaphoreType.DMA((2,))], gradient, damping, jacobi_scale,
    )
    answer = ()
    for number in range(1, ITERS):
        residual, direction, *answer = phase(
            functools.partial(middle_phase, number > 1), "middle_phase", number, n, m, (pair, pair, one), [],
            product(direction), residual, direction, scale, damp, *answer,
        )
    applied, step = phase(
        last_phase, "last_phase", ITERS, n, m, (one, tile), [], product(direction), residual, direction, scale, damp
    )
    return tuple(last_update(damping.shape, residual, direction, applied, *answer, step))


def solution(mesh):
    placed = (
        P(("lm", "kf"), None),
        P(("lm", "kf"), None, None),
        P(("lm", "kf"), None, None),
        P(("lm", "kf"), None),
        P(("lm", "kf")),
        P(None, "kf"),
        P(None, "kf"),
    )
    return jax.shard_map(
        shards,
        mesh=mesh,
        in_specs=placed,
        out_specs=(P(None, "kf"), P(None, "kf")),
        check_vma=False,
    )
```

```python
import functools

import jax
import jax.numpy as jnp
from jax import lax
from jax.experimental import pallas as pl
from jax.experimental.pallas import tpu as pltpu
from jax.sharding import PartitionSpec as P

ITERS = 2
LANES = 128
PAD = 16
SPAN = 5
CHUNK = 32
PICK = 8
DEAD = 1 << 20
LIMIT = 16 << 20


def spread_over(lifted, factors, first):
    picks = lax.broadcasted_iota(jnp.int32, lifted.shape, 0)
    half = lifted.astype(jnp.bfloat16)
    inner = jnp.zeros(lifted.shape, jnp.float32)
    for i in range(PICK):
        inner = jnp.where(picks == i, jnp.dot(half, factors[first + i], preferred_element_type=jnp.float32), inner)
    half = inner.astype(jnp.bfloat16)
    spread = jnp.zeros(lifted.shape, jnp.float32)
    for i in range(PICK):
        spread = jnp.where(
            picks == i,
            lax.dot_general(
                half, factors[first + i], (((1,), (1,)), ((), ())), preferred_element_type=jnp.float32
            ),
            spread,
        )
    return spread


def sums_of_eight(tiles):
    rows = lax.broadcasted_iota(jnp.int32, tiles[0].shape, 0)
    width = 1
    while width < PICK:
        low = (rows & width) == 0
        tiles = [
            jnp.where(low, left, right) + pltpu.roll(jnp.where(low, right, left), width, axis=0)
            for left, right in zip(tiles[::2], tiles[1::2])
        ]
        width *= 2
    return tiles[0]


def along_lanes(tile, lanes):
    dims = lax.GatherDimensionNumbers(
        offset_dims=(), collapsed_slice_dims=(1,), start_index_map=(1,),
        operand_batching_dims=(0,), start_indices_batching_dims=(0,),
    )
    return lax.gather(
        tile, lanes[..., None], dims, slice_sizes=(1, 1), mode=lax.GatherScatterMode.PROMISE_IN_BOUNDS
    )


def scatter_terms(starts, block, i, jac, row_ref, inv_ref, out_ref, even):
    terms = jac * row_ref[pl.ds(i, 1), :]
    terms = jnp.where(even, terms + pltpu.roll(terms, LANES - 1, axis=1), 0.0)
    begin = starts[block]
    for q in range(SPAN):
        lanes = jnp.broadcast_to(inv_ref[i, pl.ds(q, 1), :], terms.shape)
        out_ref[begin + q] += along_lanes(terms, lanes)


def even_lanes():
    return (lax.broadcasted_iota(jnp.int32, (PAD, LANES), 1) & 1) == 0


def product_kernel(starts, field_ref, code_ref, inv_ref, jac_ref, null_ref, out_ref, row_ref):
    out_ref[...] = jnp.zeros_like(out_ref)
    even = even_lanes()

    @pl.loop(0, null_ref.shape[0] // CHUNK)
    def _(step):
        base = pl.multiple_of(step * CHUNK, CHUNK)
        mine = pl.ds(base, CHUNK)
        codes, invs, jacs, factors = code_ref.at[mine], inv_ref.at[mine], jac_ref.at[mine], null_ref.at[mine]
        for first in range(0, CHUNK, PICK):
            tiles = []
            for i in range(first, first + PICK):
                begin = starts[base + i]
                code = jnp.broadcast_to(codes[pl.ds(i, 1), :], (PAD, LANES))
                lanes, part = code & (LANES - 1), code >> 7
                gathered = jnp.zeros((PAD, LANES), jnp.float32)
                for q in range(SPAN):
                    gathered = jnp.where(part == q, along_lanes(field_ref[begin + q], lanes), gathered)
                gathered = gathered * jacs[i]
                tiles.append(gathered[:PICK] + gathered[PICK:])
            row_ref[pl.ds(first, PICK), :] = spread_over(sums_of_eight(tiles), factors, first)
        for i in range(CHUNK):
            scatter_terms(starts, base + i, i, jacs[i], row_ref, invs, out_ref, even)


def gradient_kernel(
    starts, offs_ref, rows_ref, jac_in, null_ref, out_ref, code_ref, inv_ref, jac_ref, row_ref, slot_ref
):
    blocks = null_ref.shape[0]
    chunks = blocks // CHUNK
    out_ref[...] = jnp.zeros_like(out_ref)
    offs = offs_ref[...]
    offs = jnp.transpose(jnp.concatenate([offs] * (LANES // offs.shape[0]), axis=0))
    slot_ref[...] = offs
    lanes = lax.broadcasted_iota(jnp.int32, offs.shape, 1)
    code_ref[...] = along_lanes(offs, lanes >> 1)
    state = jac_in.shape[0]
    for c in range(PAD):
        for g in range(blocks // PICK):
            spot = pl.ds(g * PICK * PAD + c, PICK, stride=PAD)
            if c < state:
                jac_ref[spot, :] = jac_in[c, pl.ds(g * PICK, PICK), :].astype(jnp.float32)
            else:
                jac_ref[spot, :] = jnp.zeros((PICK, LANES), jnp.float32)
    even = even_lanes()
    tile = (PICK, LANES)
    target = lax.broadcasted_iota(jnp.int32, tile, 0) * LANES + lax.broadcasted_iota(jnp.int32, tile, 1)
    @pl.loop(0, chunks)
    def _(step):
        base = pl.multiple_of(step * CHUNK, CHUNK)
        mine = pl.ds(base, CHUNK)
        codes, invs, factors = code_ref.at[mine], inv_ref.at[mine], null_ref.at[mine]
        offsets = slot_ref.at[mine]
        jacs = jac_ref.at[pl.ds(pl.multiple_of(step * CHUNK * PAD, CHUNK * PAD), CHUNK * PAD)]
        residuals = rows_ref[mine, :].astype(jnp.float32)
        lifted = jnp.where(codes[...] < DEAD, residuals, 0.0)
        for first in range(0, CHUNK, PICK):
            row_ref[pl.ds(first, PICK), :] = spread_over(lifted[first:first + PICK], factors, first)
        for i in range(CHUNK):
            offset = jnp.broadcast_to(offsets[pl.ds(i, 1), :], tile)
            at = jnp.zeros(tile, jnp.int32)
            width = offs_ref.shape[0] // 2
            while width > 0:
                at = jnp.where(along_lanes(offset, at + width) <= target, at + width, at)
                width //= 2
            invs[i] = jnp.where(along_lanes(offset, at) == target, 2 * at, LANES - 1)
        for i in range(CHUNK):
            scatter_terms(starts, base + i, i, jacs[pl.ds(i * PAD, PAD), :], row_ref, invs, out_ref, even)


def local_call(kernel, name, outs, extra, in_specs, *operands):
    vmem = pl.BlockSpec(memory_space=pltpu.VMEM)
    return pl.pallas_call(
        kernel,
        in_specs=[pl.BlockSpec(memory_space=pltpu.SMEM)] + in_specs,
        out_specs=[vmem] * len(outs),
        out_shape=outs,
        scratch_shapes=[pltpu.VMEM((CHUNK, LANES), jnp.float32)] + extra,
        compiler_params=pltpu.CompilerParams(vmem_limit_bytes=LIMIT),
        name=name,
    )(*operands)


def remote(src, dst, send, recv, axis, index):
    return pltpu.make_async_remote_copy(
        src_ref=src, dst_ref=dst, send_sem=send, recv_sem=recv,
        device_id={axis: index}, device_id_type=pl.DeviceIdType.MESH,
    )


def partner(i, k):
    bit, flipped = 1, i * 0
    while bit <= k or bit == 1:
        digit = lax.rem(i // bit, 2)
        flipped = flipped + bit * ((1 - 2 * digit) if k & bit else 0)
        bit *= 2
    return i + flipped


def greet(n, m):
    i, w = lax.axis_index("lm"), lax.axis_index("kf")
    barrier = pltpu.get_barrier_semaphore()
    for k in range(n - 1, 0, -1):
        pl.semaphore_signal(
            barrier, inc=1, device_id={"lm": partner(i, k)}, device_id_type=pl.DeviceIdType.MESH
        )
    for k in range(1, m):
        pl.semaphore_signal(
            barrier, inc=1, device_id={"kf": lax.rem(w + k, m)}, device_id_type=pl.DeviceIdType.MESH
        )
    return lambda: pl.semaphore_wait(barrier, n - 1 + m - 1)


def all_reduce(n, m, pair, h, full, bufs, sems, on_shard):
    fold, acc, rs, near, far = bufs
    fold_s, fold_r, rs_s, rs_r, ag_s, ag_r, fw_s, fw_r, near_s, near_r, far_s, far_r = sems
    own = acc.shape[0]
    sh = own // n
    i, w = lax.axis_index("lm"), lax.axis_index("kf")
    later, former = lax.rem(w + 1, m), lax.rem(w + m - 1, m)

    def at(ref, j, base=0):
        return ref.at[pl.ds(base + j * sh, sh)]

    peers = [partner(i, k) for k in range(n)]
    outward = range(n - 1, 0, -1)
    across = range(n - 2, 0, -2)
    turns = [k + 1 for k in range(n - 2, -1, -2)] + [k for k in range(n - 2, -1, -2)]
    folds = {
        k: remote(at(h, peers[k], own), at(fold, peers[k]), fold_s.at[k], fold_r.at[k], "kf", later) for k in range(n)
    }

    @pl.when(w < m - 1)
    def _():
        for k in turns:
            folds[k].start()

    sends = []

    def arrived(k):
        remote(at(acc, i), rs.at[k], rs_s.at[k], rs_r.at[k], "lm", peers[1 if k % 2 else k]).wait_recv()

    for k in turns:
        spot = pl.ds(peers[k] * sh, sh)

        @pl.when(w > 0)
        def _():
            folds[k].wait_recv()
            acc[spot] = h[spot] + fold[spot]

        @pl.when(w == 0)
        def _():
            acc[spot] = h[spot]

        if k % 2 == 0:
            arrived(k + 1)
            acc[spot] += rs[k + 1]
        if k > 0:
            copy = remote(at(acc, peers[k]), rs.at[k], rs_s.at[k], rs_r.at[k], "lm", peers[1 if k % 2 else k])
            copy.start()
            sends.append(copy)
    here = pl.ds(i * sh, sh)
    total = acc[here]
    for k in range(2, n, 2):
        arrived(k)
        total = total + rs[k]
    value, products = on_shard(here, total)
    full[here] = value
    if products:
        rows = lax.broadcasted_iota(jnp.int32, near.shape[1:], 0)
        tile = jnp.zeros(near.shape[1:], jnp.float32)
        for r, product in enumerate(products):
            tile = jnp.where(rows == r, jnp.sum(jnp.sum(product, axis=0), axis=0, keepdims=True), tile)
        near[i] = tile
        for k in outward:
            copy = remote(near.at[i], near.at[i], near_s.at[k], near_r.at[k], "lm", peers[k])
            copy.start()
            sends.append(copy)
    for k in across:
        copy = remote(at(full, i), at(full, i), ag_s.at[k], ag_r.at[k], "lm", peers[k])
        copy.start()
        sends.append(copy)
    forwards = [
        remote(at(full, peers[k]), at(full, peers[k], own), fw_s.at[k], fw_r.at[k], "kf", former)
        for k in range(n if pair else 0)
    ]

    def collect(k):
        if k > 0:
            remote(
                at(full, peers[k]), at(full, peers[k]), ag_s.at[k], ag_r.at[k], "lm", peers[1 if k % 2 else k]
            ).wait_recv()
        if k % 2 == 0:
            copy = remote(
                at(full, peers[k]), at(full, peers[k]), ag_s.at[k + 1], ag_r.at[k + 1], "lm", peers[1]
            )
            copy.start()
            sends.append(copy)
        if pair:

            @pl.when(w > 0)
            def _():
                forwards[k].start()

    visits = [0] + [v for k in range(2, n, 2) for v in (k, k - 1)] + [n - 1]
    for k in visits[:n - 2]:
        collect(k)
    if products:
        for k in range(1, n):
            remote(near.at[i], near.at[peers[k]], near_s.at[k], near_r.at[k], "lm", peers[k]).wait_recv()
        tile = near[0]
        for j in range(1, n):
            tile = tile + near[j]
        far[w] = tile
        for k in range(1, m):
            copy = remote(far.at[w], far.at[w], far_s.at[k], far_r.at[w], "kf", lax.rem(w + k, m))
            copy.start()
            sends.append(copy)
    for k in visits[n - 2:]:
        collect(k)

    def sums():
        for k in range(1, m):
            j = lax.rem(w + k, m)
            remote(far.at[j], far.at[j], far_s.at[k], far_r.at[j], "kf", j).wait_recv()
        tile = far[0]
        for j in range(1, m):
            tile = tile + far[j]
        tile = jnp.sum(tile, axis=1, keepdims=True)
        return [tile[r:r + 1] for r in range(len(products))]

    def finish_pair():
        @pl.when(w < m - 1)
        def _():
            for copy in forwards:
                copy.wait_recv()

        @pl.when(w == m - 1)
        def _():
            full[pl.ds(own, own)] = jnp.zeros((own,) + full.shape[1:], jnp.float32)

    def finish_sends():
        @pl.when(w < m - 1)
        def _():
            for k in range(n):
                folds[k].wait_send()

        for copy in sends:
            copy.wait_send()
        if pair:

            @pl.when(w > 0)
            def _():
                for copy in forwards:
                    copy.wait_send()

    return sums, finish_pair, finish_sends


def columns(g):
    return pl.ds(g * LANES, LANES)


def first_phase(n, m, h, damping, jacobi_scale, res_out, dir_out, scale_out, damp_out, full, fold, acc, rs, near, far, *sems):
    own = acc.shape[0]
    sh = own // n
    state = damping.shape[0]
    i, w = lax.axis_index("lm"), lax.axis_index("kf")
    here, upper = pl.ds(0, own), pl.ds(own, own)
    met = greet(n, m)
    scale, scale_sems = sems[-2], sems[-1]
    rest = pl.ds(state, PAD - state)
    scale[here, rest, :] = jnp.zeros((own, PAD - state, LANES), jnp.float32)
    for g in range(own):
        scale[g, pl.ds(0, state), :] = jacobi_scale[:, columns(g)]
    damp_out[:, rest, :] = jnp.zeros((sh, PAD - state, LANES), jnp.float32)
    for g in range(sh):
        spot = pl.ds(pl.multiple_of((i * sh + g) * LANES, LANES), LANES)
        damp_out[g, pl.ds(0, state), :] = damping[:, spot]
    met()
    scale_copy = remote(
        scale.at[here], scale.at[upper], scale_sems.at[0], scale_sems.at[1], "kf", lax.rem(w + m - 1, m)
    )

    @pl.when(w > 0)
    def _():
        scale_copy.start()

    _, finish_pair, finish_sends = all_reduce(
        n, m, True, h, full, (fold, acc, rs, near, far), sems[:-2], lambda here, total: (-total, ())
    )

    res_out[here] = full[here]
    dir_out[here] = full[here] * scale[here]
    scale_out[here] = scale[here]

    @pl.when(w < m - 1)
    def _():
        scale_copy.wait_recv()

    @pl.when(w == m - 1)
    def _():
        scale[upper] = jnp.zeros((own,) + scale.shape[1:], jnp.float32)

    finish_pair()
    res_out[upper] = full[upper]
    dir_out[upper] = full[upper] * scale[upper]
    scale_out[upper] = scale[upper]

    @pl.when(w > 0)
    def _():
        scale_copy.wait_send()

    finish_sends()


def middle_phase(begun, n, m, h, res, direction, scale, damp, *rest):
    if begun:
        answer_in, *rest = rest
    res_out, dir_out, answer_out, full, fold, acc, rs, near, far, *sems = rest
    own = acc.shape[0]
    here = pl.ds(0, own)
    greet(n, m)()

    def on_shard(here, total):
        along, left, scaled = direction[here], res[here], scale[here]
        applied = total + damp[...] * along
        scaled_applied, scaled_left = scaled * applied, scaled * left
        return applied, (along * applied, left * scaled_applied, applied * scaled_applied, left * scaled_left)

    sums, finish_pair, finish_sends = all_reduce(
        n, m, True, h, full, (fold, acc, rs, near, far), sems, on_shard
    )
    curve, cross, square, energy = sums()
    step = energy / curve
    ratio = (energy - 2.0 * step * cross + step * step * square) / energy

    def advance(part):
        after = res[part] - step * full[part]
        res_out[part] = after
        dir_out[part] = scale[part] * after + ratio * direction[part]

    gained = step * direction[here]
    answer_out[...] = answer_in[...] + gained if begun else gained
    advance(here)
    finish_pair()
    advance(pl.ds(own, own))
    finish_sends()


def last_phase(n, m, h, res, direction, scale, damp, applied_out, step_out, full, fold, acc, rs, near, far, *sems):
    own = acc.shape[0]
    greet(n, m)()

    def on_shard(here, total):
        along, left = direction[here], res[here]
        applied = total + damp[...] * along
        return applied, (along * applied, left * left * scale[here])

    sums, _, finish_sends = all_reduce(
        n, m, False, h, full, (fold, acc, rs, near, far), sems, on_shard
    )
    curve, energy = sums()
    step_out[...] = jnp.broadcast_to(energy / curve, step_out.shape)
    applied_out[...] = full[pl.ds(0, own)]
    finish_sends()


def update_kernel(res, direction, applied, answer_in, step_in, answer_out, res_out):
    own = applied.shape[0]
    state = res_out.shape[0]
    step = step_in[pl.ds(0, 1), pl.ds(0, 1)]
    for g in range(own):
        answer_out[:, columns(g)] = (answer_in[g] + step * direction[g])[:state]
        res_out[:, columns(g)] = (res[g] - step * applied[g])[:state]


def last_update(shape, res, direction, applied, answer, step):
    half = pl.BlockSpec(applied.shape, lambda i: (0, 0, 0))
    whole = pl.BlockSpec(shape, lambda i: (0, 0))
    return pl.pallas_call(
        update_kernel,
        grid=(1,),
        in_specs=[half] * 4 + [pl.BlockSpec(step.shape, lambda i: (0, 0))],
        out_specs=[whole] * 2,
        out_shape=[jax.ShapeDtypeStruct(shape, jnp.float32)] * 2,
        compiler_params=pltpu.CompilerParams(vmem_limit_bytes=LIMIT),
        name="last_update",
    )(res, direction, applied, answer, step)


def phase(kernel, name, number, n, m, outs, extra, *operands):
    pair = operands[0].shape
    own = pair[0] // 2
    tile = pair[1:]
    vmem = pl.BlockSpec(memory_space=pltpu.VMEM)
    dma = pltpu.SemaphoreType.DMA
    return pl.pallas_call(
        functools.partial(kernel, n, m),
        in_specs=[vmem] * len(operands),
        out_specs=[vmem] * len(outs),
        out_shape=[jax.ShapeDtypeStruct(shape, jnp.float32) for shape in outs],
        scratch_shapes=[
            pltpu.VMEM(pair, jnp.float32),
            pltpu.VMEM((own,) + tile, jnp.float32),
            pltpu.VMEM((own,) + tile, jnp.float32),
            pltpu.VMEM((n, own // n) + tile, jnp.float32),
            pltpu.VMEM((n, 8, LANES), jnp.float32),
            pltpu.VMEM((m, 8, LANES), jnp.float32),
        ]
        + [dma((n,))] * 10
        + [dma((m,))] * 2
        + extra,
        compiler_params=pltpu.CompilerParams(collective_id=number, has_side_effects=True, vmem_limit_bytes=LIMIT),
        name=name,
    )(*operands)


def shards(residual_rows, jacobian, nullspace, frame_ids, obs_count, damping, jacobi_scale):
    state, frames = damping.shape
    own = frames // LANES
    blocks = nullspace.shape[0]
    ids = jnp.transpose(frame_ids) - lax.axis_index("kf") * frames
    starts = jnp.minimum(ids[0] >> 7, 2 * own - SPAN)
    slots = lax.broadcasted_iota(jnp.int32, ids.shape, 0)
    offsets = jnp.where(slots < obs_count[None, :], ids - starts[None, :] * LANES, DEAD)
    n, m = lax.axis_size("lm"), lax.axis_size("kf")
    pair, one, tile = (2 * own, PAD, LANES), (own, PAD, LANES), (8, LANES)
    vmem = pl.BlockSpec(memory_space=pltpu.VMEM)
    gradient, code, inverse, jac = local_call(
        gradient_kernel, "local_gradient",
        [
            jax.ShapeDtypeStruct(pair, jnp.float32),
            jax.ShapeDtypeStruct((blocks, LANES), jnp.int32),
            jax.ShapeDtypeStruct((blocks, PICK, LANES), jnp.int32),
            jax.ShapeDtypeStruct((blocks * PAD, LANES), jnp.float32),
        ],
        [pltpu.VMEM((blocks, LANES), jnp.int32)], [vmem] * 4,
        starts, offsets, residual_rows, jnp.transpose(jacobian, (1, 0, 2)), nullspace,
    )
    jac = jac.reshape(blocks, PAD, LANES)

    def product(field):
        return local_call(
            product_kernel, "local_field", [jax.ShapeDtypeStruct(pair, jnp.float32)], [], [vmem] * 5,
            starts, field, code, inverse, jac, nullspace,
        )[0]

    residual, direction, scale, damp = phase(
        first_phase, "first_phase", 0, n, m, (pair, pair, pair, (own // n, PAD, LANES)),
        [pltpu.VMEM(pair, jnp.float32), pltpu.SemaphoreType.DMA((2,))], gradient, damping, jacobi_scale,
    )
    answer = ()
    for number in range(1, ITERS):
        residual, direction, *answer = phase(
            functools.partial(middle_phase, number > 1), "middle_phase", number, n, m, (pair, pair, one), [],
            product(direction), residual, direction, scale, damp, *answer,
        )
    applied, step = phase(
        last_phase, "last_phase", ITERS, n, m, (one, tile), [], product(direction), residual, direction, scale, damp
    )
    return tuple(last_update(damping.shape, residual, direction, applied, *answer, step))


def solution(mesh):
    placed = (
        P(("lm", "kf"), None),
        P(("lm", "kf"), None, None),
        P(("lm", "kf"), None, None),
        P(("lm", "kf"), None),
        P(("lm", "kf")),
        P(None, "kf"),
        P(None, "kf"),
    )
    return jax.shard_map(
        shards,
        mesh=mesh,
        in_specs=placed,
        out_specs=(P(None, "kf"), P(None, "kf")),
        check_vma=False,
    )
```
